32 devices in a mesh: shot: 2 (over x), gx: 16 (over z, y, core).
Axes of the slice: x: 2, y: 2, z: 4, core: 2. Of those that a mesh axis runs over, the one named last changes fastest.
Arguments:
- waves_now: float32 [2, 1024, 64, 128], P(None, ('shot', 'gx')), parts along dimension 1, may hold values from -6 to 6
- waves_prev: float32 [2, 1024, 64, 128], P(None, ('shot', 'gx')), parts along dimension 1, may hold values from -6 to 6
- epsilon: bfloat16 [512, 64, 128], P('gx'), may hold values from 0.049804688 to 0.3984375
- tilt: bfloat16 [512, 64, 128], P('gx'), may hold values from -3.140625 to 3.140625
- azimuth: bfloat16 [512, 64, 128], P('gx'), may hold values from -3.140625 to 3.140625
- courant: bfloat16 [512, 64, 128], P('gx'), may hold values from 0.029907227 to 0.099609375
- lag_offsets: int32 [32], replicated, may hold values from -16 to 15
- table_index: int32 [128], replicated, may hold values from 0 to 3
- lag_tables: bfloat16 [4, 32, 32], replicated, may hold values from -1 to 1
Outputs:
- angle_image: bfloat16 [32, 8192, 256], P(None, ('shot', 'gx')), parts along dimension 1
The draws below stay inside these ranges and needn't reach their ends.
There are 2 independent parts, one for each index of `shot`. The reference program is written for one: setup_inputs(seed, part) draws one part's arguments, and reference() takes and returns one part's arrays. A program takes and returns all parts, laid end to end along the dimension named above; an argument that names none is the same for every part. Nothing has to cross between parts.
All inputs are finite; a program needn't handle non-finite values.
Results may differ from the reference program's by a relative error of at most 0.0049.
Values may be sent and summed in bfloat16 or wider, within the bound.
A program may use at most 64 MiB of HBM per device.

```python
import math
import jax
import jax.numpy as jnp
from jax import lax

NY = 64
NZ = 128
STEPS = 4
LAGS = 32
ANGLES = 32
LAG_REACH = 16
TABLES = 4
NX = 512


def plant(entries, rng, smallest, high):
    longest = entries.shape.index(max(entries.shape))
    spots = []
    for shift in (0, 1):
        where = [jax.random.randint(jax.random.fold_in(rng, axis), (), 0, length) for axis, length in enumerate(entries.shape)]
        where[longest] = (where[longest] + shift) % entries.shape[longest]
        spots.append(tuple(where))
    return entries.at[spots[0]].set(smallest).at[spots[1]].set(high)


def shard_levels(stream_key, dims, split, smallest, high):
    level, own = 1.0, jax.random.fold_in(stream_key, 6)
    for dim, blocks in split:
        heights = jnp.exp(jax.random.uniform(jax.random.fold_in(own, dim), (blocks,), jnp.float32, smallest / len(split), high / len(split)))
        level = level * jnp.repeat(heights, dims[dim] // blocks).reshape([-1 if axis == dim else 1 for axis in range(len(dims))])
    return level


def centred(rng, extent, spread, most, cuts=(), kind=jnp.bfloat16):
    factor_of = shard_levels(rng, extent, cuts, -0.22, 0.18) if cuts else 1.0
    array = jax.random.normal(rng, extent, jnp.float32) * spread * factor_of
    return jnp.minimum(jnp.maximum(array, -most), most).astype(kind)


def setup_inputs(seed: int = 0, part: int = 0) -> dict:
    splits = jax.random.split(jax.random.key(seed), 10)
    part_splits = jax.random.split(jax.random.fold_in(splits[9], part), 10)
    waves_now = centred(part_splits[0], (2, NX, NY, NZ), 1.0, 6.0, ((1, 16),), jnp.float32)
    waves_prev = centred(part_splits[1], (2, NX, NY, NZ), 1.0, 6.0, ((1, 16),), jnp.float32)
    epsilon = jnp.clip(0.049804688 + 0.3486328 * jax.random.uniform(splits[2], (NX, NY, NZ), jnp.float32) ** shard_levels(splits[2], (NX, NY, NZ), ((0, 16),), -0.2, 0.2), 0.049804688, 0.3984375).astype(jnp.bfloat16)
    tilt = jnp.clip(jax.random.uniform(splits[3], (NX, NY, NZ), jnp.float32, -3.140625, 3.140625), -3.140625, 3.140625).astype(jnp.bfloat16)
    azimuth = jnp.clip(jax.random.uniform(splits[4], (NX, NY, NZ), jnp.float32, -3.140625, 3.140625), -3.140625, 3.140625).astype(jnp.bfloat16)
    courant = jnp.clip(jnp.exp(math.log(0.099609375) - 1.2031561 * jax.random.uniform(splits[5], (NX, NY, NZ), jnp.float32) ** shard_levels(splits[5], (NX, NY, NZ), ((0, 16),), -0.2, 0.2)), 0.029907227, 0.099609375).astype(jnp.bfloat16)
    lag_offsets = plant(jax.random.randint(splits[6], (LAGS,), 0 - LAG_REACH, LAG_REACH), jax.random.fold_in(splits[6], 1), 0 - LAG_REACH, LAG_REACH - 1).astype(jnp.int32)
    table_index = plant(jax.random.randint(splits[7], (NZ,), 0, TABLES), jax.random.fold_in(splits[7], 1), 0, TABLES - 1).astype(jnp.int32)
    lag_tables = centred(splits[8], (TABLES, ANGLES, LAGS), LAGS ** -0.5, 1.0)
    return {"waves_now": waves_now, "waves_prev": waves_prev, "epsilon": epsilon, "tilt": tilt, "azimuth": azimuth, "courant": courant, "lag_offsets": lag_offsets, "table_index": table_index, "lag_tables": lag_tables}


def tensor(epsilon, tilt, azimuth, courant):
    eps = epsilon.astype(jnp.float32)
    theta = tilt.astype(jnp.float32)
    alpha = azimuth.astype(jnp.float32)
    speed = courant.astype(jnp.float32)
    axis_x = jnp.sin(theta) * jnp.cos(alpha)
    axis_y = jnp.sin(theta) * jnp.sin(alpha)
    axis_z = jnp.cos(theta)
    base = speed * (1.0 + 2.0 * eps)
    scaled = speed * 2.0 * eps
    return (base - scaled * axis_x * axis_x, base - scaled * axis_y * axis_y, base - scaled * axis_z * axis_z,
            -scaled * axis_x * axis_y, -scaled * axis_x * axis_z, -scaled * axis_y * axis_z)


def laplace(extended, comps):
    inner = extended.shape[1] - 2
    depth_y = extended.shape[2]
    depth_z = extended.shape[3]
    padded = jnp.pad(extended, ((0, 0), (0, 0), (1, 1), (1, 1)))

    def shifted(dx, dy, dz):
        return padded[:, 1 + dx:1 + dx + inner, 1 + dy:1 + dy + depth_y, 1 + dz:1 + dz + depth_z]

    center = shifted(0, 0, 0)
    d_xx = shifted(1, 0, 0) - 2.0 * center + shifted(-1, 0, 0)
    d_yy = shifted(0, 1, 0) - 2.0 * center + shifted(0, -1, 0)
    d_zz = shifted(0, 0, 1) - 2.0 * center + shifted(0, 0, -1)
    d_xy = shifted(1, 1, 0) - shifted(1, -1, 0) - shifted(-1, 1, 0) + shifted(-1, -1, 0)
    d_xz = shifted(1, 0, 1) - shifted(1, 0, -1) - shifted(-1, 0, 1) + shifted(-1, 0, -1)
    d_yz = shifted(0, 1, 1) - shifted(0, 1, -1) - shifted(0, -1, 1) + shifted(0, -1, -1)
    m_xx, m_yy, m_zz, m_xy, m_xz, m_yz = comps
    return (m_xx * d_xx + m_yy * d_yy + m_zz * d_zz
            + 0.5 * (m_xy * d_xy + m_xz * d_xz + m_yz * d_yz))


def reference(waves_now, waves_prev, epsilon, tilt, azimuth, courant, lag_offsets, table_index, lag_tables):
    comps = tensor(epsilon, tilt, azimuth, courant)
    current, former = waves_now, waves_prev
    for step in range(STEPS):
        extended = jnp.pad(current, ((0, 0), (1, 1), (0, 0), (0, 0)))
        following = 2.0 * current - former + laplace(extended, comps)
        former, current = current, following
    cells_x = current.shape[1]
    cells_y = current.shape[2]
    snap = current.reshape(2, cells_x // 2, 2, cells_y // 2, 2, NZ).sum(axis=(2, 4)) * 0.25
    padded = jnp.pad(snap, ((0, 0), (LAG_REACH, LAG_REACH), (0, 0), (0, 0)))
    half_x = cells_x // 2
    weights = lag_tables[table_index].astype(jnp.float32)

    def one_row(row):
        source = lax.dynamic_index_in_dim(padded[0], row, 1, keepdims=False)
        receiver = lax.dynamic_index_in_dim(padded[1], row, 1, keepdims=False)

        def one_lag(offset):
            left = lax.dynamic_slice_in_dim(source, (LAG_REACH - offset).astype(jnp.int32), half_x, 0)
            right = lax.dynamic_slice_in_dim(receiver, (LAG_REACH + offset).astype(jnp.int32), half_x, 0)
            return left * right

        lagged = jax.vmap(one_lag)(lag_offsets).astype(jnp.bfloat16)
        result = jnp.einsum('zah,hxz->azx', weights, lagged.astype(jnp.float32))
        return result.astype(jnp.bfloat16)

    rows = lax.map(one_row, jnp.arange(cells_y // 2, dtype=jnp.int32))
    return jnp.transpose(rows, (1, 0, 2, 3)).reshape(ANGLES, (cells_y // 2) * NZ, half_x)
```

```python
import functools
import jax
import jax.numpy as jnp
from jax import lax
from jax.experimental import pallas as pl
from jax.experimental.pallas import tpu as pltpu
from jax.sharding import PartitionSpec as P

STEPS = 4
LAG_REACH = 16
PAD = 8
ROWS = 8
EDGE = 32
GROUPS = 4
F32 = jnp.float32
SEND = jnp.bfloat16


def sin_cos(x):
    h = x * 0.5
    h2 = h * h
    s = h2 * 2.609020676498479e-06 + (-0.00019811149207883466)
    s = s * h2 + 0.008333088613525165
    s = s * h2 + (-0.16666660477455342)
    s = s * h2 * h + h
    c = h2 * (-2.607799327383753e-07) + 2.4761934264809493e-05
    c = c * h2 + (-0.0013888404392126607)
    c = c * h2 + 0.04166664079116777
    c = c * h2 + (-0.4999999955092854)
    c = c * h2 + 1.0
    s2 = s + s
    return s2 * c, 1.0 - s2 * s


def wave_kernel(
    n, jr, cols_per, now_hbm, prev_hbm, eps_hbm, tilt_hbm, azi_hbm, cou_hbm, cols_ref,
    buf0, buf1, sz0, sz1, dz0, dz1, eps, tilt, azi, cou, coef, zmat, pair, snap_send, sendbuf, halo,
    in_sems, prev_sem, own_sem, hs_sems, hr_sems, as_sems, ar_sems,
):
    width = eps.shape[0]
    ny = eps.shape[1]
    nz = eps.shape[2]
    half = width // 2
    chunks = ny // ROWS
    rows = pl.ds(PAD, ny)
    me = lax.axis_index("gx")
    has_low = me > 0
    has_high = me < n - 1
    bufs = (buf0, buf1)
    szs = (sz0, sz1)
    dzs = (dz0, dz1)
    group = width // GROUPS

    def group_copies(g):
        part = pl.ds(g * group, group)
        pairs = (
            (tilt_hbm.at[part], tilt.at[part]),
            (azi_hbm.at[part], azi.at[part]),
            (eps_hbm.at[part], eps.at[part]),
            (cou_hbm.at[part], cou.at[part]),
            (now_hbm.at[:, part], buf0.at[:, part, rows, :]),
        )
        return [
            pltpu.make_async_copy(src, dst, in_sems.at[g, k]) for k, (src, dst) in enumerate(pairs)
        ]

    for g in range(GROUPS):
        for copy in group_copies(g):
            copy.start()
    prev_copy = pltpu.make_async_copy(prev_hbm, buf1.at[:, :, rows, :], prev_sem)
    prev_copy.start()

    barrier = pltpu.get_barrier_semaphore()

    def greet(k, carry):
        pl.semaphore_signal(
            barrier, inc=1, device_id={"gx": lax.rem(me + k, n)},
            device_id_type=pl.DeviceIdType.MESH,
        )
        return carry

    lax.fori_loop(1, n, greet, 0)

    zero_rows = jnp.zeros((2, width, PAD, nz), F32)
    for ref in (buf0, buf1, dz0, dz1):
        ref[:, :, pl.ds(0, PAD), :] = zero_rows
        ref[:, :, pl.ds(PAD + ny, PAD), :] = zero_rows
    zero_ends = jnp.zeros((STEPS, 2, 2, PAD, nz), F32)
    halo[:, :, :, pl.ds(0, PAD), :] = zero_ends
    halo[:, :, :, pl.ds(PAD + ny, PAD), :] = zero_ends
    for side, has in ((0, has_low), (1, has_high)):
        @pl.when(jnp.logical_not(has))
        def _(side=side):
            halo[:, side, :, rows, :] = jnp.zeros((STEPS, 2, ny, nz), F32)

    r = lax.broadcasted_iota(jnp.int32, (nz, 2 * nz), 0)
    c = lax.broadcasted_iota(jnp.int32, (nz, 2 * nz), 1)
    second = c < nz
    cz = jnp.where(second, c, c - nz)
    zmat[...] = jnp.where(
        r == cz + 1, 1.0,
        jnp.where(r == cz - 1, jnp.where(second, 1.0, -1.0),
                  jnp.where((r == cz) & second, -2.0, 0.0)),
    ).astype(jnp.bfloat16)

    def halo_copy(step, side):
        if step == 0:
            src = now_hbm.at[:, 0 if side == 0 else width - 1]
        else:
            src = sendbuf.at[step - 1, side]
        return pltpu.make_async_remote_copy(
            src_ref=src,
            dst_ref=halo.at[step, 1 - side, :, rows, :],
            send_sem=hs_sems.at[step, side],
            recv_sem=hr_sems.at[step, 1 - side],
            device_id={"gx": me - 1 if side == 0 else me + 1},
            device_id_type=pl.DeviceIdType.MESH,
        )

    def halo_arrived(step, side):
        return pltpu.make_async_remote_copy(
            src_ref=sendbuf.at[0, side],
            dst_ref=halo.at[step, side, :, rows, :],
            send_sem=hs_sems.at[step, side],
            recv_sem=hr_sems.at[step, side],
            device_id={"gx": me - 1 if side == 0 else me + 1},
            device_id_type=pl.DeviceIdType.MESH,
        )

    def send_halo(step):
        for side, has in ((0, has_low), (1, has_high)):
            @pl.when(has)
            def _(side=side):
                halo_copy(step, side).start()

    def z_terms(p):
        return jnp.dot(p.astype(jnp.bfloat16), zmat[...], preferred_element_type=F32)

    def prepare(x, carry):
        found = z_terms(buf0[:, x, rows, :].reshape(2 * ny, nz))
        theta_s, theta_c = sin_cos(tilt[x].astype(F32))
        alpha_s, alpha_c = sin_cos(azi[x].astype(F32))
        speed = cou[x].astype(F32)
        e2 = eps[x].astype(F32) * 2.0
        scaled = speed * e2
        base = speed + scaled
        nx = theta_s * alpha_c
        nyy = theta_s * alpha_s
        sx = scaled * nx
        sy = scaled * nyy
        scz = scaled * theta_c
        mxx = base - sx * nx
        myy = base - sy * nyy
        coef[0, x] = mxx
        coef[1, x] = myy
        coef[2, x] = base - scz * theta_c
        coef[3, x] = -0.5 * (sx * nyy)
        coef[4, x] = -0.5 * (scz * nx)
        coef[5, x] = -0.5 * (scz * nyy)
        coef[6, x] = 2.0 - 2.0 * (mxx + myy)
        sz0[:, x, rows, :] = found[:, :nz].reshape(2, ny, nz)
        dz0[:, x, rows, :] = found[:, nz:].reshape(2, ny, nz)
        return carry

    for g in range(GROUPS):
        for copy in group_copies(g):
            copy.wait()
        lax.fori_loop(g * group, (g + 1) * group, prepare, 0)
        if g == 0:
            pl.semaphore_wait(barrier, n - 1)
            send_halo(0)
    prev_copy.wait()

    def combine(cs, p, old, px, sy, sz, yx, dzx, dzy):
        acc = cs[6] * p - old
        acc += cs[0] * px + cs[1] * sy
        acc += cs[2] * sz + cs[3] * yx
        acc += cs[4] * dzx + cs[5] * dzy
        return acc

    def edges(step):
        now, prv = bufs[step % 2], bufs[(step + 1) % 2]
        sz, dz = szs[step % 2], dzs[step % 2]
        for side, has in ((0, has_low), (1, has_high)):
            @pl.when(has)
            def _(side=side):
                halo_arrived(step, side).wait_recv()
        both = [halo[step, side, f, rows, :] for side in range(2) for f in range(2)]
        outer = jnp.dot(
            jnp.concatenate(both, axis=0).astype(jnp.bfloat16), zmat[:, nz:],
            preferred_element_type=F32,
        )
        for side in range(2):
            x = 0 if side == 0 else width - 1
            inner = 1 if side == 0 else width - 2
            for y in range(0, ny, EDGE):
                mid, up, dn = [pl.ds(PAD + y + d, EDGE) for d in (0, 1, -1)]
                cs = [coef[k, x, pl.ds(y, EDGE), :] for k in range(7)]
                for f in range(2):
                    a = halo[step, side, f, mid, :]
                    ya = halo[step, side, f, up, :] - halo[step, side, f, dn, :]
                    first = (side * 2 + f) * ny + y
                    za = outer[first : first + EDGE]
                    b = now[f, inner, mid, :]
                    yb = now[f, inner, up, :] - now[f, inner, dn, :]
                    zb = dz[f, inner, mid, :]
                    acc = combine(
                        cs, now[f, x, mid, :], prv[f, x, mid, :], a + b,
                        now[f, x, up, :] + now[f, x, dn, :], sz[f, x, mid, :],
                        yb - ya if side == 0 else ya - yb,
                        zb - za if side == 0 else za - zb,
                        dz[f, x, up, :] - dz[f, x, dn, :],
                    )
                    prv[f, x, mid, :] = acc
                    if step < STEPS - 1:
                        sendbuf[step, side, f, pl.ds(y, EDGE), :] = acc
        if step < STEPS - 1:
            send_halo(step + 1)

    def inside(step, base, emit):
        now, prv = bufs[step % 2], bufs[(step + 1) % 2]
        sz, dz = szs[step % 2], dzs[step % 2]
        mid, up, dn = [pl.ds(base + PAD + d, ROWS) for d in (0, 1, -1)]
        here = pl.ds(base, ROWS)
        p0, y0, d0, p1, y1, s1, d1 = [[None, None] for _ in range(7)]
        for f in range(2):
            p0[f] = now[f, 0, mid, :]
            y0[f] = now[f, 0, up, :] - now[f, 0, dn, :]
            d0[f] = dz[f, 0, mid, :]
            hi, lo = now[f, 1, up, :], now[f, 1, dn, :]
            p1[f], y1[f], s1[f], d1[f] = now[f, 1, mid, :], hi - lo, hi + lo, dz[f, 1, mid, :]
        for x in range(1, width - 1):
            cs = [coef[k, x, here, :] for k in range(7)]
            for f in range(2):
                hi, lo = now[f, x + 1, up, :], now[f, x + 1, dn, :]
                p2, y2, s2, d2 = now[f, x + 1, mid, :], hi - lo, hi + lo, dz[f, x + 1, mid, :]
                acc = combine(
                    cs, p1[f], prv[f, x, mid, :], p2 + p0[f], s1[f], sz[f, x, mid, :],
                    y2 - y0[f], d2 - d0[f], dz[f, x, up, :] - dz[f, x, dn, :],
                )
                emit(f, x, mid, acc)
                p0[f], y0[f], d0[f] = p1[f], y1[f], d1[f]
                p1[f], y1[f], s1[f], d1[f] = p2, y2, s2, d2

    def z_rows(step, base):
        prv, sz, dz = bufs[(step + 1) % 2], szs[(step + 1) % 2], dzs[(step + 1) % 2]
        at = pl.ds(base, ROWS)
        found = z_terms(jnp.concatenate([prv[f, x, at, :] for x in range(width) for f in range(2)], axis=0))
        for x in range(width):
            for f in range(2):
                first = (x * 2 + f) * ROWS
                sz[f, x, at, :] = found[first : first + ROWS, :nz]
                dz[f, x, at, :] = found[first : first + ROWS, nz:]

    for step in range(STEPS - 1):
        edges(step)

        def emit(f, x, mid, acc, prv=bufs[(step + 1) % 2]):
            prv[f, x, mid, :] = acc

        def advance(k, carry, step=step, emit=emit):
            base = pl.multiple_of(k * ROWS, ROWS)
            z_rows(step, base)
            inside(step, base, emit)
            return carry

        lax.fori_loop(0, chunks, advance, 0)
        z_rows(step, ny)

    edges(STEPS - 1)
    final = bufs[STEPS % 2]
    span = jr * half
    each = n // chunks

    def piece(target, source):
        start = pl.multiple_of(((target * cols_per) // nz) * half, half)
        return pltpu.make_async_remote_copy(
            src_ref=snap_send.at[:, pl.ds(start, span), :],
            dst_ref=cols_ref.at[source],
            send_sem=as_sems.at[target],
            recv_sem=ar_sems.at[source],
            device_id={"gx": target},
            device_id_type=pl.DeviceIdType.MESH,
        )

    start = pl.multiple_of(((me * cols_per) // nz) * half, half)
    own = pltpu.make_async_copy(snap_send.at[:, pl.ds(start, span), :], cols_ref.at[me], own_sem)

    def last(k, carry):
        away = (k + 1) // 2
        away = jnp.where(lax.rem(k, 2) == 1, chunks // 2 - away, chunks // 2 + away)
        block = lax.rem(me // each + away, chunks)
        base = pl.multiple_of(block * ROWS, ROWS)
        mid = pl.ds(base + PAD, ROWS)
        held = [final[f, 0, mid, :] for f in range(2)]

        def emit(f, x, mid, acc):
            if x % 2 == 0:
                held[f] = acc
            else:
                pair[f, pl.ds((x // 2) * ROWS, ROWS), :] = held[f] + acc

        inside(STEPS - 1, base, emit)
        for f in range(2):
            pair[f, pl.ds((half - 1) * ROWS, ROWS), :] = held[f] + final[f, width - 1, mid, :]
        for f in range(2):
            for j in range(ROWS // 2):
                even = pair[f, pl.ds(2 * j, half, stride=ROWS), :]
                odd = pair[f, pl.ds(2 * j + 1, half, stride=ROWS), :]
                at = pl.multiple_of((block * (ROWS // 2) + j) * half, half)
                snap_send[f, pl.ds(at, half), :] = ((even + odd) * 0.25).astype(SEND)

        def send(u, carry):
            target = block * each + u

            @pl.when(target != me)
            def _():
                piece(target, me).start()

            return carry

        lax.fori_loop(0, each, send, 0)
        return carry

    lax.fori_loop(0, chunks, last, 0)
    own.start()

    for step in range(STEPS):
        for side, has in ((0, has_low), (1, has_high)):
            @pl.when(has)
            def _(step=step, side=side):
                halo_copy(step, side).wait_send()

    def wait_piece(k, carry):
        piece(lax.rem(me + k, n), me).wait_send()
        piece(lax.rem(me + k, n), lax.rem(me + k, n)).wait_recv()
        return carry

    lax.fori_loop(1, n, wait_piece, 0)
    own.wait()


def image_kernel(
    cols_per, jr, offsets, tables_at, cols_ref, tab_ref, out_ref, lines, wide, prods
):
    n = cols_ref.shape[0]
    half = cols_ref.shape[2] // jr
    nz = cols_ref.shape[3]
    full = n * half
    step = pl.program_id(0)
    tables = tab_ref.shape[0]
    angles = tab_ref.shape[1]
    lags = tab_ref.shape[2]

    @pl.when(step == 0)
    def _():
        for f in range(2):
            for j in range(jr):
                for t in range(full // nz):
                    per = nz // half
                    block = cols_ref[pl.ds(t * per, per), f, pl.ds(j * half, half), :]
                    block = block.reshape(nz, nz).astype(F32)
                    lines[f, j, :, pl.ds(t * nz, nz)] = block.T.astype(SEND)
        lag = lax.broadcasted_iota(jnp.int32, (lags, lags * 8), 0)
        col = lax.broadcasted_iota(jnp.int32, (lags, lags * 8), 1)
        spread = jnp.where(col // 8 == lag, 1.0, 0.0).astype(jnp.bfloat16)
        flat = tab_ref[...].reshape(tables * angles, lags)
        wide[...] = jnp.dot(flat, spread, preferred_element_type=F32).astype(jnp.bfloat16)

    me = lax.axis_index("gx")
    z0 = lax.rem(me * cols_per, nz)
    lane = lax.broadcasted_iota(jnp.int32, (16, nz), 1)
    tiles = full // nz
    ta = tables * angles
    sub = lax.broadcasted_iota(jnp.int32, (8, ta), 0)
    row_c = lax.rem(lax.broadcasted_iota(jnp.int32, (angles * 8, lags * 8), 0), 8)
    col_c = lax.rem(lax.broadcasted_iota(jnp.int32, (angles * 8, lags * 8), 1), 8)
    diagonal = row_c == col_c
    lane_ta = lax.broadcasted_iota(jnp.int32, (angles, 8, ta), 2)
    row_a = lax.broadcasted_iota(jnp.int32, (angles, 8, ta), 0)
    weights = []
    for q in range(2):
        row0 = z0 + step * 16 + q * 8
        chosen = jnp.zeros((8, ta), jnp.int32)
        for c in range(8):
            chosen = jnp.where(sub == c, tables_at[row0 + c], chosen)
        wanted = (chosen * angles)[None] + row_a
        pick = jnp.where(lane_ta == wanted, 1.0, 0.0).reshape(angles * 8, ta)
        dense = jnp.dot(pick.astype(jnp.bfloat16), wide[...], preferred_element_type=F32)
        weights.append(jnp.where(diagonal, dense, 0.0).astype(jnp.bfloat16))

    def moved(parts, d):
        if d == 0:
            return [part.astype(F32) for part in parts]
        turned = [pltpu.roll(part, d % nz, axis=1).astype(F32) for part in parts]
        zero = jnp.zeros((16, nz), F32)
        if d > 0:
            return [
                jnp.where(lane >= d, turned[t], turned[t - 1] if t else zero)
                for t in range(tiles)
            ]
        return [
            jnp.where(lane < nz + d, turned[t], turned[t + 1] if t + 1 < tiles else zero)
            for t in range(tiles)
        ]

    for j in range(jr):
        results = []
        row0 = pl.multiple_of(z0 + step * 16, 16)
        source = [lines[0, j, pl.ds(row0, 16), pl.ds(t * nz, nz)] for t in range(tiles)]
        receiver = [lines[1, j, pl.ds(row0, 16), pl.ds(t * nz, nz)] for t in range(tiles)]
        for d in range(-LAG_REACH, LAG_REACH):
            left, right = moved(source, d), moved(receiver, -d)
            for t in range(tiles):
                product = left[t] * right[t]
                for q in range(2):
                    prods[j * 2 + q, d + LAG_REACH, :, pl.ds(t * nz, nz)] = product[8 * q : 8 * q + 8]
        for q in range(2):
            slot = j * 2 + q
            lagged = jnp.concatenate(
                [prods[slot, offsets[h] + LAG_REACH] for h in range(lags)], axis=0
            ).astype(jnp.bfloat16)
            total = jnp.dot(weights[q], lagged, preferred_element_type=F32)
            results.append(total.reshape(angles, 8, full))
        both = jnp.concatenate(results, axis=1)
        out_ref[:, j] = both.astype(jnp.bfloat16)


def local(
    waves_now, waves_prev, epsilon, tilt, azimuth, courant, lag_offsets, table_index, lag_tables
):
    n = lax.axis_size("gx")
    width, ny, nz = epsilon.shape
    half = width // 2
    columns = (ny // 2) * nz
    cols_per = columns // n
    jr = max(1, cols_per // nz)
    full = n * half
    plane = (2, width, ny + 2 * PAD, nz)
    dma = pltpu.SemaphoreType.DMA
    cols = pl.pallas_call(
        functools.partial(wave_kernel, n, jr, cols_per),
        out_shape=jax.ShapeDtypeStruct((n, 2, jr * half, nz), SEND),
        in_specs=[pl.BlockSpec(memory_space=pltpu.HBM)] * 6,
        out_specs=pl.BlockSpec(memory_space=pltpu.VMEM),
        scratch_shapes=[
            pltpu.VMEM(plane, F32),
            pltpu.VMEM(plane, F32),
            pltpu.VMEM(plane, F32),
            pltpu.VMEM(plane, F32),
            pltpu.VMEM(plane, F32),
            pltpu.VMEM(plane, F32),
            pltpu.VMEM((width, ny, nz), epsilon.dtype),
            pltpu.VMEM((width, ny, nz), tilt.dtype),
            pltpu.VMEM((width, ny, nz), azimuth.dtype),
            pltpu.VMEM((width, ny, nz), courant.dtype),
            pltpu.VMEM((7, width, ny, nz), F32),
            pltpu.VMEM((nz, 2 * nz), jnp.bfloat16),
            pltpu.VMEM((2, half * ROWS, nz), F32),
            pltpu.VMEM((2, (ny // 2) * half, nz), SEND),
            pltpu.VMEM((STEPS - 1, 2, 2, ny, nz), F32),
            pltpu.VMEM((STEPS, 2, 2, ny + 2 * PAD, nz), F32),
            dma((GROUPS, 5)),
            dma,
            dma,
            dma((STEPS, 2)),
            dma((STEPS, 2)),
            dma((n,)),
            dma((n,)),
        ],
        compiler_params=pltpu.CompilerParams(
            collective_id=0, has_side_effects=True, vmem_limit_bytes=60 << 20
        ),
        name="waves",
    )(waves_now, waves_prev, epsilon, tilt, azimuth, courant)

    angles, lags = lag_tables.shape[1:]
    tables = lag_tables.shape[0]
    cz = min(cols_per, nz)
    image = pl.pallas_call(
        functools.partial(image_kernel, cols_per, jr),
        grid=(cz // 16,),
        out_shape=jax.ShapeDtypeStruct((angles, jr, cz, full), jnp.bfloat16),
        in_specs=[
            pl.BlockSpec(memory_space=pltpu.SMEM),
            pl.BlockSpec(memory_space=pltpu.SMEM),
            pl.BlockSpec(memory_space=pltpu.VMEM),
            pl.BlockSpec(memory_space=pltpu.VMEM),
        ],
        out_specs=pl.BlockSpec((angles, jr, 16, full), lambda g: (0, 0, g, 0)),
        scratch_shapes=[
            pltpu.VMEM((2, jr, nz, full), SEND),
            pltpu.VMEM((tables * angles, lags * 8), jnp.bfloat16),
            pltpu.VMEM((jr * 2, 2 * LAG_REACH, 8, full), F32),
        ],
        compiler_params=pltpu.CompilerParams(vmem_limit_bytes=60 << 20),
        name="image",
    )(lag_offsets, table_index, cols, lag_tables)
    return image.reshape(angles, cols_per, full)


def solution(mesh):
    wave = P(None, ("shot", "gx"), None, None)
    cell = P("gx", None, None)
    return jax.shard_map(
        local,
        mesh=mesh,
        in_specs=(wave, wave, cell, cell, cell, cell, P(), P(), P()),
        out_specs=P(None, ("shot", "gx"), None),
        check_vma=False,
    )
```

```python
import functools
import jax
import jax.numpy as jnp
from jax import lax
from jax.experimental import pallas as pl
from jax.experimental.pallas import tpu as pltpu
from jax.sharding import PartitionSpec as P

STEPS = 4
LAG_REACH = 16
PAD = 16
ROWS = 8
DEPTH = 32
TALL = 16
EDGE = 32
GROUPS = 4
F32 = jnp.float32
SEND = jnp.bfloat16


def sin_cos(x):
    u = x * x
    s = u * 7.206469580499954e-09 - 2.1888434293738905e-06
    s = s * u + 0.00036827396667825314
    s = s * u - 0.029462771608356236
    s = s * u + 0.7071067811865476
    s = s * x
    c = u * -3.6015480241538463e-10 + 1.3679165339017438e-07
    c = c * u - 3.0689327892292986e-05
    c = c * u + 0.003682845531587343
    c = c * u - 0.17677669370892954
    c = c * u + 1.4142135623730951
    return s * c, 1.0 - s * s


def wave_kernel(
    n, jr, cols_per, now_hbm, prev_hbm, eps_hbm, tilt_hbm, azi_hbm, cou_hbm, cols_ref,
    buf0, buf1, sz0, sz1, dz0, dz1, eps, tilt, azi, cou, coef, zmat, pair, snap_send, sendbuf, halo,
    in_sems, prev_sem, own_sem, hs_sems, hr_sems, as_sems, ar_sems,
):
    width = eps.shape[0]
    ny = eps.shape[1]
    nz = eps.shape[2]
    half = width // 2
    chunks = ny // ROWS
    rows = pl.ds(PAD, ny)
    me = lax.axis_index("gx")
    has_low = me > 0
    has_high = me < n - 1
    bufs = (buf0, buf1)
    szs = (sz0, sz1)
    dzs = (dz0, dz1)
    group = width // GROUPS

    def group_copies(g):
        part = pl.ds(g * group, group)
        pairs = (
            (tilt_hbm.at[part], tilt.at[part]),
            (azi_hbm.at[part], azi.at[part]),
            (eps_hbm.at[part], eps.at[part]),
            (cou_hbm.at[part], cou.at[part]),
            (now_hbm.at[:, part], buf0.at[:, part, rows, :]),
        )
        return [
            pltpu.make_async_copy(src, dst, in_sems.at[g, k]) for k, (src, dst) in enumerate(pairs)
        ]

    for g in range(GROUPS):
        for copy in group_copies(g):
            copy.start()
    prev_copy = pltpu.make_async_copy(prev_hbm, buf1.at[:, :, rows, :], prev_sem)
    prev_copy.start()

    barrier = pltpu.get_barrier_semaphore()

    def greet(k, carry):
        pl.semaphore_signal(
            barrier, inc=1, device_id={"gx": lax.rem(me + k, n)},
            device_id_type=pl.DeviceIdType.MESH,
        )
        return carry

    lax.fori_loop(1, n, greet, 0)

    zero_rows = jnp.zeros((2, width, PAD, nz), F32)
    for ref in (buf0, buf1, dz0, dz1):
        ref[:, :, pl.ds(0, PAD), :] = zero_rows
        ref[:, :, pl.ds(PAD + ny, PAD), :] = zero_rows
    zero_ends = jnp.zeros((STEPS, 2, 2, PAD, nz), F32)
    halo[:, :, :, pl.ds(0, PAD), :] = zero_ends
    halo[:, :, :, pl.ds(PAD + ny, PAD), :] = zero_ends
    for side, has in ((0, has_low), (1, has_high)):
        @pl.when(jnp.logical_not(has))
        def _(side=side):
            halo[:, side, :, rows, :] = jnp.zeros((STEPS, 2, ny, nz), F32)

    r = lax.broadcasted_iota(jnp.int32, (nz, 2 * nz), 0)
    c = lax.broadcasted_iota(jnp.int32, (nz, 2 * nz), 1)
    second = c < nz
    cz = jnp.where(second, c, c - nz)
    zmat[...] = jnp.where(
        r == cz + 1, 1.0,
        jnp.where(r == cz - 1, jnp.where(second, 1.0, -1.0),
                  jnp.where((r == cz) & second, -2.0, 0.0)),
    ).astype(jnp.bfloat16)

    def halo_copy(step, side):
        if step == 0:
            src = now_hbm.at[:, 0 if side == 0 else width - 1]
        else:
            src = sendbuf.at[step - 1, side]
        return pltpu.make_async_remote_copy(
            src_ref=src,
            dst_ref=halo.at[step, 1 - side, :, rows, :],
            send_sem=hs_sems.at[step, side],
            recv_sem=hr_sems.at[step, 1 - side],
            device_id={"gx": me - 1 if side == 0 else me + 1},
            device_id_type=pl.DeviceIdType.MESH,
        )

    def halo_arrived(step, side):
        return pltpu.make_async_remote_copy(
            src_ref=sendbuf.at[0, side],
            dst_ref=halo.at[step, side, :, rows, :],
            send_sem=hs_sems.at[step, side],
            recv_sem=hr_sems.at[step, side],
            device_id={"gx": me - 1 if side == 0 else me + 1},
            device_id_type=pl.DeviceIdType.MESH,
        )

    def send_halo(step):
        for side, has in ((0, has_low), (1, has_high)):
            @pl.when(has)
            def _(side=side):
                halo_copy(step, side).start()

    def z_terms(p):
        return jnp.dot(p.astype(jnp.bfloat16), zmat[...], preferred_element_type=F32)

    def prepare(x, carry):
        found = z_terms(buf0[:, x, rows, :].reshape(2 * ny, nz))
        theta_s, theta_c = sin_cos(tilt[x].astype(F32))
        alpha_s, alpha_c = sin_cos(azi[x].astype(F32))
        speed = cou[x].astype(F32)
        e2 = eps[x].astype(F32) * 2.0
        scaled = speed * e2
        base = speed + scaled
        nx = theta_s * alpha_c
        nyy = theta_s * alpha_s
        sx = scaled * nx
        sy = scaled * nyy
        scz = scaled * theta_c
        mxx = base - sx * nx
        myy = base - sy * nyy
        coef[0, x] = mxx
        coef[1, x] = myy
        coef[2, x] = base - scz * theta_c
        coef[3, x] = -0.5 * (sx * nyy)
        coef[4, x] = -0.5 * (scz * nx)
        coef[5, x] = -0.5 * (scz * nyy)
        coef[6, x] = 2.0 - 2.0 * (mxx + myy)
        sz0[:, x, rows, :] = found[:, :nz].reshape(2, ny, nz)
        dz0[:, x, rows, :] = found[:, nz:].reshape(2, ny, nz)
        return carry

    for g in range(GROUPS):
        for copy in group_copies(g):
            copy.wait()
        lax.fori_loop(g * group, (g + 1) * group, prepare, 0)
        if g == 0:
            pl.semaphore_wait(barrier, n - 1)
            send_halo(0)
    prev_copy.wait()

    def combine(cs, p, old, px, sy, sz, yx, dzx, dzy):
        acc = cs[6] * p - old
        acc += cs[0] * px + cs[1] * sy
        acc += cs[2] * sz + cs[3] * yx
        acc += cs[4] * dzx + cs[5] * dzy
        return acc

    def edges(step):
        now, prv = bufs[step % 2], bufs[(step + 1) % 2]
        sz, dz = szs[step % 2], dzs[step % 2]
        for side, has in ((0, has_low), (1, has_high)):
            @pl.when(has)
            def _(side=side):
                halo_arrived(step, side).wait_recv()
        both = [halo[step, side, f, rows, :] for side in range(2) for f in range(2)]
        outer = jnp.dot(
            jnp.concatenate(both, axis=0).astype(jnp.bfloat16), zmat[:, nz:],
            preferred_element_type=F32,
        )
        for side in range(2):
            x = 0 if side == 0 else width - 1
            inner = 1 if side == 0 else width - 2
            for y in range(0, ny, EDGE):
                mid, up, dn = [pl.ds(PAD + y + d, EDGE) for d in (0, 1, -1)]
                cs = [coef[k, x, pl.ds(y, EDGE), :] for k in range(7)]
                for f in range(2):
                    a = halo[step, side, f, mid, :]
                    ya = halo[step, side, f, up, :] - halo[step, side, f, dn, :]
                    first = (side * 2 + f) * ny + y
                    za = outer[first : first + EDGE]
                    b = now[f, inner, mid, :]
                    yb = now[f, inner, up, :] - now[f, inner, dn, :]
                    zb = dz[f, inner, mid, :]
                    acc = combine(
                        cs, now[f, x, mid, :], prv[f, x, mid, :], a + b,
                        now[f, x, up, :] + now[f, x, dn, :], sz[f, x, mid, :],
                        yb - ya if side == 0 else ya - yb,
                        zb - za if side == 0 else za - zb,
                        dz[f, x, up, :] - dz[f, x, dn, :],
                    )
                    prv[f, x, mid, :] = acc
                    if step < STEPS - 1:
                        sendbuf[step, side, f, pl.ds(y, EDGE), :] = acc
        if step < STEPS - 1:
            send_halo(step + 1)

    def inside(step, base, emit, tall):
        now, prv = bufs[step % 2], bufs[(step + 1) % 2]
        sz, dz = szs[step % 2], dzs[step % 2]
        mid, up, dn = [pl.ds(base + PAD + d, tall) for d in (0, 1, -1)]
        here = pl.ds(base, tall)
        p0, y0, d0, p1, y1, s1, d1 = [[None, None] for _ in range(7)]
        for f in range(2):
            p0[f] = now[f, 0, mid, :]
            y0[f] = now[f, 0, up, :] - now[f, 0, dn, :]
            d0[f] = dz[f, 0, mid, :]
            hi, lo = now[f, 1, up, :], now[f, 1, dn, :]
            p1[f], y1[f], s1[f], d1[f] = now[f, 1, mid, :], hi - lo, hi + lo, dz[f, 1, mid, :]
        for x in range(1, width - 1):
            cs = [coef[k, x, here, :] for k in range(7)]
            for f in range(2):
                hi, lo = now[f, x + 1, up, :], now[f, x + 1, dn, :]
                p2, y2, s2, d2 = now[f, x + 1, mid, :], hi - lo, hi + lo, dz[f, x + 1, mid, :]
                acc = combine(
                    cs, p1[f], prv[f, x, mid, :], p2 + p0[f], s1[f], sz[f, x, mid, :],
                    y2 - y0[f], d2 - d0[f], dz[f, x, up, :] - dz[f, x, dn, :],
                )
                emit(f, x, mid, acc)
                p0[f], y0[f], d0[f] = p1[f], y1[f], d1[f]
                p1[f], y1[f], s1[f], d1[f] = p2, y2, s2, d2

    def z_rows(step, base):
        prv, sz, dz = bufs[(step + 1) % 2], szs[(step + 1) % 2], dzs[(step + 1) % 2]
        at = pl.ds(base, TALL)
        found = z_terms(jnp.concatenate([prv[f, x, at, :] for x in range(width) for f in range(2)], axis=0))
        for x in range(width):
            for f in range(2):
                first = (x * 2 + f) * TALL
                sz[f, x, at, :] = found[first : first + TALL, :nz]
                dz[f, x, at, :] = found[first : first + TALL, nz:]

    for step in range(STEPS - 1):
        edges(step)

        def emit(f, x, mid, acc, prv=bufs[(step + 1) % 2]):
            prv[f, x, mid, :] = acc

        def advance(k, carry, step=step, emit=emit):
            base = pl.multiple_of(k * TALL, TALL)
            z_rows(step, base + PAD - TALL)
            inside(step, base, emit, TALL)
            return carry

        lax.fori_loop(0, ny // TALL, advance, 0)
        z_rows(step, PAD + ny - TALL)

    edges(STEPS - 1)
    final = bufs[STEPS % 2]
    span = jr * half
    each = n // chunks

    def piece(target, source):
        start = pl.multiple_of(((target * cols_per) // nz) * half, half)
        return pltpu.make_async_remote_copy(
            src_ref=snap_send.at[:, pl.ds(start, span), :],
            dst_ref=cols_ref.at[source],
            send_sem=as_sems.at[target],
            recv_sem=ar_sems.at[source],
            device_id={"gx": target},
            device_id_type=pl.DeviceIdType.MESH,
        )

    start = pl.multiple_of(((me * cols_per) // nz) * half, half)
    own = pltpu.make_async_copy(snap_send.at[:, pl.ds(start, span), :], cols_ref.at[me], own_sem)

    def last(k, carry):
        mine = me // each
        low = 2 * mine < chunks
        near = jnp.where(low, mine, chunks - 1 - mine)
        lead = chunks - 1 - 2 * near
        rest = jnp.maximum(k - lead, 0)
        pick = jnp.where(lax.rem(rest, 2) == 0, 2 * near - rest // 2, rest // 2)
        pick = jnp.where(k < lead, chunks - 1 - k, pick)
        block = jnp.where(low, pick, chunks - 1 - pick)
        base = pl.multiple_of(block * ROWS, ROWS)
        mid = pl.ds(base + PAD, ROWS)
        held = [final[f, 0, mid, :] for f in range(2)]

        def emit(f, x, mid, acc):
            if x % 2 == 0:
                held[f] = acc
            else:
                pair[f, pl.ds((x // 2) * ROWS, ROWS), :] = held[f] + acc

        inside(STEPS - 1, base, emit, ROWS)
        for f in range(2):
            pair[f, pl.ds((half - 1) * ROWS, ROWS), :] = held[f] + final[f, width - 1, mid, :]
        for f in range(2):
            for j in range(ROWS // 2):
                even = pair[f, pl.ds(2 * j, half, stride=ROWS), :]
                odd = pair[f, pl.ds(2 * j + 1, half, stride=ROWS), :]
                at = pl.multiple_of((block * (ROWS // 2) + j) * half, half)
                snap_send[f, pl.ds(at, half), :] = ((even + odd) * 0.25).astype(SEND)

        def send(u, carry):
            target = block * each + u

            @pl.when(target != me)
            def _():
                piece(target, me).start()

            return carry

        lax.fori_loop(0, each, send, 0)
        return carry

    lax.fori_loop(0, chunks, last, 0)
    own.start()

    for step in range(STEPS):
        for side, has in ((0, has_low), (1, has_high)):
            @pl.when(has)
            def _(step=step, side=side):
                halo_copy(step, side).wait_send()

    def wait_piece(k, carry):
        piece(lax.rem(me + k, n), me).wait_send()
        piece(lax.rem(me + k, n), lax.rem(me + k, n)).wait_recv()
        return carry

    lax.fori_loop(1, n, wait_piece, 0)
    own.wait()


def image_kernel(
    cols_per, jr, offsets, tables_at, cols_ref, tab_ref, out_ref, lines, wide, keep, prods
):
    n = cols_ref.shape[0]
    half = cols_ref.shape[2] // jr
    nz = cols_ref.shape[3]
    full = n * half
    step = pl.program_id(0)
    blocks = pl.num_programs(0) - 1
    tables = tab_ref.shape[0]
    angles = tab_ref.shape[1]
    lags = tab_ref.shape[2]

    @pl.when(step == 0)
    def _():
        for f in range(2):
            for j in range(jr):
                for t in range(full // nz):
                    per = nz // half
                    block = cols_ref[pl.ds(t * per, per), f, pl.ds(j * half, half), :]
                    block = block.reshape(nz, nz).astype(F32)
                    lines[f, j, :, pl.ds(t * nz, nz)] = block.T.astype(SEND)
        lag = lax.broadcasted_iota(jnp.int32, (lags, lags * 8), 0)
        col = lax.broadcasted_iota(jnp.int32, (lags, lags * 8), 1)
        spread = jnp.where(col // 8 == lag, 1.0, 0.0).astype(jnp.bfloat16)
        flat = tab_ref[...].reshape(tables * angles, lags)
        wide[...] = jnp.dot(flat, spread, preferred_element_type=F32).astype(jnp.bfloat16)
        row_c = lax.rem(lax.broadcasted_iota(jnp.int32, (angles * 8, lags * 8), 0), 8)
        col_c = lax.rem(lax.broadcasted_iota(jnp.int32, (angles * 8, lags * 8), 1), 8)
        keep[...] = jnp.where(row_c == col_c, 1.0, 0.0).astype(jnp.bfloat16)

    me = lax.axis_index("gx")
    z0 = lax.rem(me * cols_per, nz)
    tiles = full // nz
    ta = tables * angles
    slot = lax.rem(step, 2)
    before = 1 - slot

    sub = lax.broadcasted_iota(jnp.int32, (8, ta), 0)
    lane_ta = lax.broadcasted_iota(jnp.int32, (angles, 8, ta), 2)
    row_a = lax.broadcasted_iota(jnp.int32, (angles, 8, ta), 0)
    weights = []
    for q in range(DEPTH // 8):
        row0 = z0 + jnp.maximum(step - 1, 0) * DEPTH + q * 8
        chosen = jnp.zeros((8, ta), jnp.int32)
        for c in range(8):
            chosen = jnp.where(sub == c, tables_at[row0 + c], chosen)
        wanted = (chosen * angles)[None] + row_a
        pick = jnp.where(lane_ta == wanted, 1.0, 0.0).reshape(angles * 8, ta)
        dense = jnp.dot(pick.astype(jnp.bfloat16), wide[...], preferred_element_type=F32)
        weights.append(dense.astype(jnp.bfloat16) * keep[...])

    for j in range(jr):
        results = []
        for q in range(DEPTH // 8):
            lagged = jnp.concatenate(
                [prods[before, j * (DEPTH // 8) + q, offsets[h] + LAG_REACH] for h in range(lags)], axis=0
            ).astype(jnp.bfloat16)
            total = jnp.dot(weights[q], lagged, preferred_element_type=F32)
            results.append(total.reshape(angles, 8, full))
        out_ref[:, j] = jnp.concatenate(results, axis=1).astype(jnp.bfloat16)

    lane = lax.broadcasted_iota(jnp.int16, (DEPTH, nz), 1)
    zero = jnp.zeros((DEPTH, nz), SEND)

    def moved(parts, d):
        if d == 0:
            return parts
        turned = [pltpu.roll(part, d % nz, axis=1) for part in parts]
        if d > 0:
            return [
                jnp.where(lane >= d, turned[t], turned[t - 1] if t else zero)
                for t in range(tiles)
            ]
        return [
            jnp.where(lane < nz + d, turned[t], turned[t + 1] if t + 1 < tiles else zero)
            for t in range(tiles)
        ]

    row0 = pl.multiple_of(z0 + jnp.minimum(step, blocks - 1) * DEPTH, DEPTH)
    for j in range(jr):
        source = [lines[0, j, pl.ds(row0, DEPTH), pl.ds(t * nz, nz)] for t in range(tiles)]
        receiver = [lines[1, j, pl.ds(row0, DEPTH), pl.ds(t * nz, nz)] for t in range(tiles)]
        for d in range(-LAG_REACH, LAG_REACH):
            left, right = moved(source, d), moved(receiver, -d)
            for t in range(tiles):
                product = (left[t] * right[t]).astype(F32)
                for q in range(DEPTH // 8):
                    prods[slot, j * (DEPTH // 8) + q, d + LAG_REACH, :, pl.ds(t * nz, nz)] = product[8 * q : 8 * q + 8]


def local(
    waves_now, waves_prev, epsilon, tilt, azimuth, courant, lag_offsets, table_index, lag_tables
):
    n = lax.axis_size("gx")
    width, ny, nz = epsilon.shape
    half = width // 2
    columns = (ny // 2) * nz
    cols_per = columns // n
    jr = max(1, cols_per // nz)
    full = n * half
    plane = (2, width, ny + 2 * PAD, nz)
    dma = pltpu.SemaphoreType.DMA
    cols = pl.pallas_call(
        functools.partial(wave_kernel, n, jr, cols_per),
        out_shape=jax.ShapeDtypeStruct((n, 2, jr * half, nz), SEND),
        in_specs=[pl.BlockSpec(memory_space=pltpu.HBM)] * 6,
        out_specs=pl.BlockSpec(memory_space=pl.ANY),
        scratch_shapes=[
            pltpu.VMEM(plane, F32),
            pltpu.VMEM(plane, F32),
            pltpu.VMEM(plane, F32),
            pltpu.VMEM(plane, F32),
            pltpu.VMEM(plane, F32),
            pltpu.VMEM(plane, F32),
            pltpu.VMEM((width, ny, nz), epsilon.dtype),
            pltpu.VMEM((width, ny, nz), tilt.dtype),
            pltpu.VMEM((width, ny, nz), azimuth.dtype),
            pltpu.VMEM((width, ny, nz), courant.dtype),
            pltpu.VMEM((7, width, ny, nz), F32),
            pltpu.VMEM((nz, 2 * nz), jnp.bfloat16),
            pltpu.VMEM((2, half * ROWS, nz), F32),
            pltpu.VMEM((2, (ny // 2) * half, nz), SEND),
            pltpu.VMEM((STEPS - 1, 2, 2, ny, nz), F32),
            pltpu.VMEM((STEPS, 2, 2, ny + 2 * PAD, nz), F32),
            dma((GROUPS, 5)),
            dma,
            dma,
            dma((STEPS, 2)),
            dma((STEPS, 2)),
            dma((n,)),
            dma((n,)),
        ],
        compiler_params=pltpu.CompilerParams(
            collective_id=0, has_side_effects=True, vmem_limit_bytes=60 << 20
        ),
        name="waves",
    )(waves_now, waves_prev, epsilon, tilt, azimuth, courant)

    angles, lags = lag_tables.shape[1:]
    tables = lag_tables.shape[0]
    cz = min(cols_per, nz)
    image = pl.pallas_call(
        functools.partial(image_kernel, cols_per, jr),
        grid=(cz // DEPTH + 1,),
        out_shape=jax.ShapeDtypeStruct((angles, jr, cz, full), jnp.bfloat16),
        in_specs=[
            pl.BlockSpec(memory_space=pltpu.SMEM),
            pl.BlockSpec(memory_space=pltpu.SMEM),
            pl.BlockSpec(memory_space=pltpu.VMEM),
            pl.BlockSpec(memory_space=pltpu.VMEM),
        ],
        out_specs=pl.BlockSpec((angles, jr, DEPTH, full), lambda g: (0, 0, jnp.maximum(g - 1, 0), 0)),
        scratch_shapes=[
            pltpu.VMEM((2, jr, nz, full), SEND),
            pltpu.VMEM((tables * angles, lags * 8), jnp.bfloat16),
            pltpu.VMEM((angles * 8, lags * 8), jnp.bfloat16),
            pltpu.VMEM((2, jr * (DEPTH // 8), 2 * LAG_REACH, 8, full), F32),
        ],
        compiler_params=pltpu.CompilerParams(vmem_limit_bytes=60 << 20),
        name="image",
    )(lag_offsets, table_index, cols, lag_tables)
    return image.reshape(angles, cols_per, full)


def solution(mesh):
    wave = P(None, ("shot", "gx"), None, None)
    cell = P("gx", None, None)
    return jax.shard_map(
        local,
        mesh=mesh,
        in_specs=(wave, wave, cell, cell, cell, cell, P(), P(), P()),
        out_specs=P(None, ("shot", "gx"), None),
        check_vma=False,
    )
```

```python
import functools
import jax
import jax.numpy as jnp
from jax import lax
from jax.experimental import pallas as pl
from jax.experimental.pallas import tpu as pltpu
from jax.sharding import PartitionSpec as P

STEPS = 4
LAG_REACH = 16
PAD = 16
ROWS = 8
DEPTH = 32
TALL = 16
EDGE = 32
GROUPS = 4
F32 = jnp.float32
SEND = jnp.bfloat16


def sin_cos(x):
    u = x * x
    s = u * 7.206469580499954e-09 - 2.1888434293738905e-06
    s = s * u + 0.00036827396667825314
    s = s * u - 0.029462771608356236
    s = s * u + 0.7071067811865476
    s = s * x
    c = u * -3.6015480241538463e-10 + 1.3679165339017438e-07
    c = c * u - 3.0689327892292986e-05
    c = c * u + 0.003682845531587343
    c = c * u - 0.17677669370892954
    c = c * u + 1.4142135623730951
    return s * c, 1.0 - s * s


def wave_kernel(
    n, jr, cols_per, now_hbm, prev_hbm, eps_hbm, tilt_hbm, azi_hbm, cou_hbm, cols_ref,
    buf0, buf1, sz0, sz1, dz0, dz1, eps, tilt, azi, cou, coef, zmat, pair, snap_send, sendbuf, halo,
    in_sems, prev_sem, own_sem, hs_sems, hr_sems, as_sems, ar_sems,
):
    width = eps.shape[0]
    ny = eps.shape[1]
    nz = eps.shape[2]
    half = width // 2
    chunks = ny // ROWS
    rows = pl.ds(PAD, ny)
    me = lax.axis_index("gx")
    has_low = me > 0
    has_high = me < n - 1
    bufs = (buf0, buf1)
    szs = (sz0, sz1)
    dzs = (dz0, dz1)
    group = width // GROUPS

    def group_copies(g):
        part = pl.ds(g * group, group)
        pairs = (
            (tilt_hbm.at[part], tilt.at[part]),
            (azi_hbm.at[part], azi.at[part]),
            (eps_hbm.at[part], eps.at[part]),
            (cou_hbm.at[part], cou.at[part]),
            (now_hbm.at[:, part], buf0.at[:, part, rows, :]),
        )
        return [
            pltpu.make_async_copy(src, dst, in_sems.at[g, k]) for k, (src, dst) in enumerate(pairs)
        ]

    for g in range(GROUPS):
        for copy in group_copies(g):
            copy.start()
    prev_copy = pltpu.make_async_copy(prev_hbm, buf1.at[:, :, rows, :], prev_sem)
    prev_copy.start()

    barrier = pltpu.get_barrier_semaphore()

    def greet(k, carry):
        pl.semaphore_signal(
            barrier, inc=1, device_id={"gx": lax.rem(me + k, n)},
            device_id_type=pl.DeviceIdType.MESH,
        )
        return carry

    lax.fori_loop(1, n, greet, 0)

    zero_rows = jnp.zeros((2, width, PAD, nz), F32)
    for ref in (buf0, buf1, dz0, dz1):
        ref[:, :, pl.ds(0, PAD), :] = zero_rows
        ref[:, :, pl.ds(PAD + ny, PAD), :] = zero_rows
    zero_ends = jnp.zeros((STEPS, 2, 2, PAD, nz), F32)
    halo[:, :, :, pl.ds(0, PAD), :] = zero_ends
    halo[:, :, :, pl.ds(PAD + ny, PAD), :] = zero_ends
    for side, has in ((0, has_low), (1, has_high)):
        @pl.when(jnp.logical_not(has))
        def _(side=side):
            halo[:, side, :, rows, :] = jnp.zeros((STEPS, 2, ny, nz), F32)

    r = lax.broadcasted_iota(jnp.int32, (nz, 2 * nz), 0)
    c = lax.broadcasted_iota(jnp.int32, (nz, 2 * nz), 1)
    second = c < nz
    cz = jnp.where(second, c, c - nz)
    zmat[...] = jnp.where(
        r == cz + 1, 1.0,
        jnp.where(r == cz - 1, jnp.where(second, 1.0, -1.0),
                  jnp.where((r == cz) & second, -2.0, 0.0)),
    ).astype(jnp.bfloat16)

    def halo_copy(step, side):
        if step == 0:
            src = now_hbm.at[:, 0 if side == 0 else width - 1]
        else:
            src = sendbuf.at[step - 1, side]
        return pltpu.make_async_remote_copy(
            src_ref=src,
            dst_ref=halo.at[step, 1 - side, :, rows, :],
            send_sem=hs_sems.at[step, side],
            recv_sem=hr_sems.at[step, 1 - side],
            device_id={"gx": me - 1 if side == 0 else me + 1},
            device_id_type=pl.DeviceIdType.MESH,
        )

    def halo_arrived(step, side):
        return pltpu.make_async_remote_copy(
            src_ref=sendbuf.at[0, side],
            dst_ref=halo.at[step, side, :, rows, :],
            send_sem=hs_sems.at[step, side],
            recv_sem=hr_sems.at[step, side],
            device_id={"gx": me - 1 if side == 0 else me + 1},
            device_id_type=pl.DeviceIdType.MESH,
        )

    def send_halo(step):
        for side, has in ((0, has_low), (1, has_high)):
            @pl.when(has)
            def _(side=side):
                halo_copy(step, side).start()

    def z_terms(p):
        return jnp.dot(p.astype(jnp.bfloat16), zmat[...], preferred_element_type=F32)

    def prepare(x, carry):
        found = z_terms(buf0[:, x, rows, :].reshape(2 * ny, nz))
        theta_s, theta_c = sin_cos(tilt[x].astype(F32))
        alpha_s, alpha_c = sin_cos(azi[x].astype(F32))
        speed = cou[x].astype(F32)
        e2 = eps[x].astype(F32) * 2.0
        scaled = speed * e2
        base = speed + scaled
        nx = theta_s * alpha_c
        nyy = theta_s * alpha_s
        sx = scaled * nx
        sy = scaled * nyy
        scz = scaled * theta_c
        mxx = base - sx * nx
        myy = base - sy * nyy
        coef[0, x] = mxx
        coef[1, x] = myy
        coef[2, x] = base - scz * theta_c
        coef[3, x] = -0.5 * (sx * nyy)
        coef[4, x] = -0.5 * (scz * nx)
        coef[5, x] = -0.5 * (scz * nyy)
        coef[6, x] = 2.0 - 2.0 * (mxx + myy)
        sz0[:, x, rows, :] = found[:, :nz].reshape(2, ny, nz)
        dz0[:, x, rows, :] = found[:, nz:].reshape(2, ny, nz)
        return carry

    for g in range(GROUPS):
        for copy in group_copies(g):
            copy.wait()
        lax.fori_loop(g * group, (g + 1) * group, prepare, 0, unroll=4)
        if g == 0:
            pl.semaphore_wait(barrier, n - 1)
            send_halo(0)
    prev_copy.wait()

    def combine(cs, p, old, px, sy, sz, yx, dzx, dzy):
        acc = cs[6] * p - old
        acc += cs[0] * px + cs[1] * sy
        acc += cs[2] * sz + cs[3] * yx
        acc += cs[4] * dzx + cs[5] * dzy
        return acc

    def edges(step):
        now, prv = bufs[step % 2], bufs[(step + 1) % 2]
        sz, dz = szs[step % 2], dzs[step % 2]
        for side, has in ((0, has_low), (1, has_high)):
            @pl.when(has)
            def _(side=side):
                halo_arrived(step, side).wait_recv()
        both = [halo[step, side, f, rows, :] for side in range(2) for f in range(2)]
        outer = jnp.dot(
            jnp.concatenate(both, axis=0).astype(jnp.bfloat16), zmat[:, nz:],
            preferred_element_type=F32,
        )
        for side in range(2):
            x = 0 if side == 0 else width - 1
            inner = 1 if side == 0 else width - 2
            for y in range(0, ny, EDGE):
                mid, up, dn = [pl.ds(PAD + y + d, EDGE) for d in (0, 1, -1)]
                cs = [coef[k, x, pl.ds(y, EDGE), :] for k in range(7)]
                for f in range(2):
                    a = halo[step, side, f, mid, :]
                    ya = halo[step, side, f, up, :] - halo[step, side, f, dn, :]
                    first = (side * 2 + f) * ny + y
                    za = outer[first : first + EDGE]
                    b = now[f, inner, mid, :]
                    yb = now[f, inner, up, :] - now[f, inner, dn, :]
                    zb = dz[f, inner, mid, :]
                    acc = combine(
                        cs, now[f, x, mid, :], prv[f, x, mid, :], a + b,
                        now[f, x, up, :] + now[f, x, dn, :], sz[f, x, mid, :],
                        yb - ya if side == 0 else ya - yb,
                        zb - za if side == 0 else za - zb,
                        dz[f, x, up, :] - dz[f, x, dn, :],
                    )
                    prv[f, x, mid, :] = acc
                    if step < STEPS - 1:
                        sendbuf[step, side, f, pl.ds(y, EDGE), :] = acc
        if step < STEPS - 1:
            send_halo(step + 1)

    def inside(step, base, emit, tall):
        now, prv = bufs[step % 2], bufs[(step + 1) % 2]
        sz, dz = szs[step % 2], dzs[step % 2]
        mid, up, dn = [pl.ds(base + PAD + d, tall) for d in (0, 1, -1)]
        here = pl.ds(base, tall)
        p0, y0, d0, p1, y1, s1, d1 = [[None, None] for _ in range(7)]
        for f in range(2):
            p0[f] = now[f, 0, mid, :]
            y0[f] = now[f, 0, up, :] - now[f, 0, dn, :]
            d0[f] = dz[f, 0, mid, :]
            hi, lo = now[f, 1, up, :], now[f, 1, dn, :]
            p1[f], y1[f], s1[f], d1[f] = now[f, 1, mid, :], hi - lo, hi + lo, dz[f, 1, mid, :]
        for x in range(1, width - 1):
            cs = [coef[k, x, here, :] for k in range(7)]
            for f in range(2):
                hi, lo = now[f, x + 1, up, :], now[f, x + 1, dn, :]
                p2, y2, s2, d2 = now[f, x + 1, mid, :], hi - lo, hi + lo, dz[f, x + 1, mid, :]
                acc = combine(
                    cs, p1[f], prv[f, x, mid, :], p2 + p0[f], s1[f], sz[f, x, mid, :],
                    y2 - y0[f], d2 - d0[f], dz[f, x, up, :] - dz[f, x, dn, :],
                )
                emit(f, x, mid, acc)
                p0[f], y0[f], d0[f] = p1[f], y1[f], d1[f]
                p1[f], y1[f], s1[f], d1[f] = p2, y2, s2, d2

    def z_rows(step, base):
        prv, sz, dz = bufs[(step + 1) % 2], szs[(step + 1) % 2], dzs[(step + 1) % 2]
        at = pl.ds(base, TALL)
        found = z_terms(jnp.concatenate([prv[f, x, at, :] for x in range(width) for f in range(2)], axis=0))
        for x in range(width):
            for f in range(2):
                first = (x * 2 + f) * TALL
                sz[f, x, at, :] = found[first : first + TALL, :nz]
                dz[f, x, at, :] = found[first : first + TALL, nz:]

    for step in range(STEPS - 1):
        edges(step)

        def emit(f, x, mid, acc, prv=bufs[(step + 1) % 2]):
            prv[f, x, mid, :] = acc

        def advance(k, carry, step=step, emit=emit):
            base = pl.multiple_of(k * TALL, TALL)
            z_rows(step, base + PAD - TALL)
            inside(step, base, emit, TALL)
            return carry

        lax.fori_loop(0, ny // TALL, advance, 0)
        z_rows(step, PAD + ny - TALL)

    edges(STEPS - 1)
    final = bufs[STEPS % 2]
    span = jr * half
    each = n // chunks

    def piece(target, source):
        start = pl.multiple_of(((target * cols_per) // nz) * half, half)
        return pltpu.make_async_remote_copy(
            src_ref=snap_send.at[:, pl.ds(start, span), :],
            dst_ref=cols_ref.at[source],
            send_sem=as_sems.at[target],
            recv_sem=ar_sems.at[source],
            device_id={"gx": target},
            device_id_type=pl.DeviceIdType.MESH,
        )

    start = pl.multiple_of(((me * cols_per) // nz) * half, half)
    own = pltpu.make_async_copy(snap_send.at[:, pl.ds(start, span), :], cols_ref.at[me], own_sem)

    def last(k, carry):
        mine = me // each
        low = 2 * mine < chunks
        near = jnp.where(low, mine, chunks - 1 - mine)
        lead = chunks - 1 - 2 * near
        rest = jnp.maximum(k - lead, 0)
        pick = jnp.where(lax.rem(rest, 2) == 0, 2 * near - rest // 2, rest // 2)
        pick = jnp.where(k < lead, chunks - 1 - k, pick)
        block = jnp.where(low, pick, chunks - 1 - pick)
        base = pl.multiple_of(block * ROWS, ROWS)
        mid = pl.ds(base + PAD, ROWS)
        held = [final[f, 0, mid, :] for f in range(2)]

        def emit(f, x, mid, acc):
            if x % 2 == 0:
                held[f] = acc
            else:
                pair[f, pl.ds((x // 2) * ROWS, ROWS), :] = held[f] + acc

        inside(STEPS - 1, base, emit, ROWS)
        for f in range(2):
            pair[f, pl.ds((half - 1) * ROWS, ROWS), :] = held[f] + final[f, width - 1, mid, :]
        for f in range(2):
            for j in range(ROWS // 2):
                even = pair[f, pl.ds(2 * j, half, stride=ROWS), :]
                odd = pair[f, pl.ds(2 * j + 1, half, stride=ROWS), :]
                at = pl.multiple_of((block * (ROWS // 2) + j) * half, half)
                snap_send[f, pl.ds(at, half), :] = ((even + odd) * 0.25).astype(SEND)

        def send(u, carry):
            target = block * each + u

            @pl.when(target != me)
            def _():
                piece(target, me).start()

            return carry

        lax.fori_loop(0, each, send, 0)
        return carry

    lax.fori_loop(0, chunks, last, 0)
    own.start()

    for step in range(STEPS):
        for side, has in ((0, has_low), (1, has_high)):
            @pl.when(has)
            def _(step=step, side=side):
                halo_copy(step, side).wait_send()

    def wait_piece(k, carry):
        piece(lax.rem(me + k, n), me).wait_send()
        piece(lax.rem(me + k, n), lax.rem(me + k, n)).wait_recv()
        return carry

    lax.fori_loop(1, n, wait_piece, 0)
    own.wait()


def image_kernel(
    cols_per, jr, offsets, tables_at, cols_ref, tab_ref, out_ref, lines, wide, keep, *prods
):
    n = cols_ref.shape[0]
    half = cols_ref.shape[2] // jr
    nz = cols_ref.shape[3]
    full = n * half
    step = pl.program_id(0)
    tables = tab_ref.shape[0]
    angles = tab_ref.shape[1]
    lags = tab_ref.shape[2]

    @pl.when(step == 0)
    def _():
        for f in range(2):
            for j in range(jr):
                for t in range(full // nz):
                    per = nz // half
                    block = cols_ref[pl.ds(t * per, per), f, pl.ds(j * half, half), :]
                    block = block.reshape(nz, nz).astype(F32)
                    lines[f, j, :, pl.ds(t * nz, nz)] = block.T.astype(SEND)
        lag = lax.broadcasted_iota(jnp.int32, (lags, lags * 8), 0)
        col = lax.broadcasted_iota(jnp.int32, (lags, lags * 8), 1)
        spread = jnp.where(col // 8 == lag, 1.0, 0.0).astype(jnp.bfloat16)
        flat = tab_ref[...].reshape(tables * angles, lags)
        wide[...] = jnp.dot(flat, spread, preferred_element_type=F32).astype(jnp.bfloat16)
        row_c = lax.rem(lax.broadcasted_iota(jnp.int32, (angles * 8, lags * 8), 0), 8)
        col_c = lax.rem(lax.broadcasted_iota(jnp.int32, (angles * 8, lags * 8), 1), 8)
        keep[...] = jnp.where(row_c == col_c, 1.0, 0.0).astype(jnp.bfloat16)

    me = lax.axis_index("gx")
    z0 = lax.rem(me * cols_per, nz)
    tiles = full // nz
    ta = tables * angles

    sub = lax.broadcasted_iota(jnp.int32, (8, ta), 0)
    lane_ta = lax.broadcasted_iota(jnp.int32, (angles, 8, ta), 2)
    row_a = lax.broadcasted_iota(jnp.int32, (angles, 8, ta), 0)
    weights = []
    for q in range(DEPTH // 8):
        row0 = z0 + step * DEPTH + q * 8
        chosen = jnp.zeros((8, ta), jnp.int32)
        for c in range(8):
            chosen = jnp.where(sub == c, tables_at[row0 + c], chosen)
        wanted = (chosen * angles)[None] + row_a
        pick = jnp.where(lane_ta == wanted, 1.0, 0.0).reshape(angles * 8, ta)
        dense = jnp.dot(pick.astype(jnp.bfloat16), wide[...], preferred_element_type=F32)
        weights.append(dense.astype(jnp.bfloat16) * keep[...])

    lane = lax.broadcasted_iota(jnp.int16, (DEPTH, nz), 1)
    zero = jnp.zeros((DEPTH, nz), SEND)

    def moved(parts, d):
        if d == 0:
            return parts
        turned = [pltpu.roll(part, d % nz, axis=1) for part in parts]
        if d > 0:
            return [
                jnp.where(lane >= d, turned[t], turned[t - 1] if t else zero)
                for t in range(tiles)
            ]
        return [
            jnp.where(lane < nz + d, turned[t], turned[t + 1] if t + 1 < tiles else zero)
            for t in range(tiles)
        ]

    row0 = pl.multiple_of(z0 + step * DEPTH, DEPTH)
    for j in range(jr):
        source = [lines[0, j, pl.ds(row0, DEPTH), pl.ds(t * nz, nz)] for t in range(tiles)]
        receiver = [lines[1, j, pl.ds(row0, DEPTH), pl.ds(t * nz, nz)] for t in range(tiles)]
        for d in range(-LAG_REACH, LAG_REACH):
            left, right = moved(source, d), moved(receiver, -d)
            for t in range(tiles):
                product = (left[t] * right[t]).astype(F32)
                for q in range(DEPTH // 8):
                    prods[j * (DEPTH // 8) + q][d + LAG_REACH, :, pl.ds(t * nz, nz)] = product[8 * q : 8 * q + 8]

    for j in range(jr):
        results = []
        for q in range(DEPTH // 8):
            lagged = jnp.concatenate(
                [prods[j * (DEPTH // 8) + q][offsets[h] + LAG_REACH] for h in range(lags)], axis=0
            ).astype(jnp.bfloat16)
            total = jnp.dot(weights[q], lagged, preferred_element_type=F32)
            results.append(total.reshape(angles, 8, full))
        out_ref[:, j] = jnp.concatenate(results, axis=1).astype(jnp.bfloat16)


def local(
    waves_now, waves_prev, epsilon, tilt, azimuth, courant, lag_offsets, table_index, lag_tables
):
    n = lax.axis_size("gx")
    width, ny, nz = epsilon.shape
    half = width // 2
    columns = (ny // 2) * nz
    cols_per = columns // n
    jr = max(1, cols_per // nz)
    full = n * half
    plane = (2, width, ny + 2 * PAD, nz)
    dma = pltpu.SemaphoreType.DMA
    cols = pl.pallas_call(
        functools.partial(wave_kernel, n, jr, cols_per),
        out_shape=jax.ShapeDtypeStruct((n, 2, jr * half, nz), SEND),
        in_specs=[pl.BlockSpec(memory_space=pltpu.HBM)] * 6,
        out_specs=pl.BlockSpec(memory_space=pl.ANY),
        scratch_shapes=[
            pltpu.VMEM(plane, F32),
            pltpu.VMEM(plane, F32),
            pltpu.VMEM(plane, F32),
            pltpu.VMEM(plane, F32),
            pltpu.VMEM(plane, F32),
            pltpu.VMEM(plane, F32),
            pltpu.VMEM((width, ny, nz), epsilon.dtype),
            pltpu.VMEM((width, ny, nz), tilt.dtype),
            pltpu.VMEM((width, ny, nz), azimuth.dtype),
            pltpu.VMEM((width, ny, nz), courant.dtype),
            pltpu.VMEM((7, width, ny, nz), F32),
            pltpu.VMEM((nz, 2 * nz), jnp.bfloat16),
            pltpu.VMEM((2, half * ROWS, nz), F32),
            pltpu.VMEM((2, (ny // 2) * half, nz), SEND),
            pltpu.VMEM((STEPS - 1, 2, 2, ny, nz), F32),
            pltpu.VMEM((STEPS, 2, 2, ny + 2 * PAD, nz), F32),
            dma((GROUPS, 5)),
            dma,
            dma,
            dma((STEPS, 2)),
            dma((STEPS, 2)),
            dma((n,)),
            dma((n,)),
        ],
        compiler_params=pltpu.CompilerParams(
            collective_id=0, has_side_effects=True, vmem_limit_bytes=60 << 20
        ),
        name="waves",
    )(waves_now, waves_prev, epsilon, tilt, azimuth, courant)

    angles, lags = lag_tables.shape[1:]
    tables = lag_tables.shape[0]
    cz = min(cols_per, nz)
    image = pl.pallas_call(
        functools.partial(image_kernel, cols_per, jr),
        grid=(cz // DEPTH,),
        out_shape=jax.ShapeDtypeStruct((angles, jr, cz, full), jnp.bfloat16),
        in_specs=[
            pl.BlockSpec(memory_space=pltpu.SMEM),
            pl.BlockSpec(memory_space=pltpu.SMEM),
            pl.BlockSpec(memory_space=pltpu.VMEM),
            pl.BlockSpec(memory_space=pltpu.VMEM),
        ],
        out_specs=pl.BlockSpec((angles, jr, DEPTH, full), lambda g: (0, 0, g, 0)),
        scratch_shapes=[
            pltpu.VMEM((2, jr, nz, full), SEND),
            pltpu.VMEM((tables * angles, lags * 8), jnp.bfloat16),
            pltpu.VMEM((angles * 8, lags * 8), jnp.bfloat16),
        ] + [pltpu.VMEM((2 * LAG_REACH, 8, full), F32)] * (jr * (DEPTH // 8)),
        compiler_params=pltpu.CompilerParams(vmem_limit_bytes=60 << 20),
        name="image",
    )(lag_offsets, table_index, cols, lag_tables)
    return image.reshape(angles, cols_per, full)


def solution(mesh):
    wave = P(None, ("shot", "gx"), None, None)
    cell = P("gx", None, None)
    return jax.shard_map(
        local,
        mesh=mesh,
        in_specs=(wave, wave, cell, cell, cell, cell, P(), P(), P()),
        out_specs=P(None, ("shot", "gx"), None),
        check_vma=False,
    )
```

```python
import functools
import jax
import jax.numpy as jnp
from jax import lax
from jax.experimental import pallas as pl
from jax.experimental.pallas import tpu as pltpu
from jax.sharding import PartitionSpec as P

STEPS = 4
LAG_REACH = 16
PAD = 16
ROWS = 8
DEPTH = 32
TALL = 16
EDGE = 32
GROUPS = 4
F32 = jnp.float32
SEND = jnp.bfloat16


def sin_cos(x):
    u = x * x
    s = u * 7.206469580499954e-09 - 2.1888434293738905e-06
    s = s * u + 0.00036827396667825314
    s = s * u - 0.029462771608356236
    s = s * u + 0.7071067811865476
    s = s * x
    c = u * -3.6015480241538463e-10 + 1.3679165339017438e-07
    c = c * u - 3.0689327892292986e-05
    c = c * u + 0.003682845531587343
    c = c * u - 0.17677669370892954
    c = c * u + 1.4142135623730951
    return s * c, 1.0 - s * s


def wave_kernel(
    n, jr, cols_per, now_hbm, prev_hbm, eps_hbm, tilt_hbm, azi_hbm, cou_hbm, cols_ref,
    buf0, buf1, sz0, sz1, dz0, dz1, eps, tilt, azi, cou, coef, zmat, pair, snap_send, sendbuf, halo, arrived,
    in_sems, prev_sem, own_sem, hs_sems, hr_sems, as_sems, ar_sems,
):
    width = eps.shape[0]
    ny = eps.shape[1]
    nz = eps.shape[2]
    half = width // 2
    chunks = ny // ROWS
    rows = pl.ds(PAD, ny)
    me = lax.axis_index("gx")
    has_low = me > 0
    has_high = me < n - 1
    bufs = (buf0, buf1)
    szs = (sz0, sz1)
    dzs = (dz0, dz1)
    group = width // GROUPS

    def group_copies(g):
        part = pl.ds(g * group, group)
        pairs = (
            (tilt_hbm.at[part], tilt.at[part]),
            (azi_hbm.at[part], azi.at[part]),
            (eps_hbm.at[part], eps.at[part]),
            (cou_hbm.at[part], cou.at[part]),
            (now_hbm.at[:, part], buf0.at[:, part, rows, :]),
        )
        return [
            pltpu.make_async_copy(src, dst, in_sems.at[g, k]) for k, (src, dst) in enumerate(pairs)
        ]

    for g in range(GROUPS):
        for copy in group_copies(g):
            copy.start()
    prev_copy = pltpu.make_async_copy(prev_hbm, buf1.at[:, :, rows, :], prev_sem)
    prev_copy.start()

    barrier = pltpu.get_barrier_semaphore()

    def greet(k, carry):
        pl.semaphore_signal(
            barrier, inc=1, device_id={"gx": lax.rem(me + k, n)},
            device_id_type=pl.DeviceIdType.MESH,
        )
        return carry

    lax.fori_loop(1, n, greet, 0)

    zero_rows = jnp.zeros((2, width, PAD, nz), F32)
    for ref in (buf0, buf1, dz0, dz1):
        ref[:, :, pl.ds(0, PAD), :] = zero_rows
        ref[:, :, pl.ds(PAD + ny, PAD), :] = zero_rows
    zero_ends = jnp.zeros((2, 2, PAD, nz), F32)
    halo[:, :, pl.ds(0, PAD), :] = zero_ends
    halo[:, :, pl.ds(PAD + ny, PAD), :] = zero_ends
    for side, has in ((0, has_low), (1, has_high)):
        @pl.when(jnp.logical_not(has))
        def _(side=side):
            halo[side, :, rows, :] = jnp.zeros((2, ny, nz), F32)
            arrived[:, side] = jnp.zeros((STEPS - 1, 2, ny, nz), SEND)

    r = lax.broadcasted_iota(jnp.int32, (nz, 2 * nz), 0)
    c = lax.broadcasted_iota(jnp.int32, (nz, 2 * nz), 1)
    second = c < nz
    cz = jnp.where(second, c, c - nz)
    zmat[...] = jnp.where(
        r == cz + 1, 1.0,
        jnp.where(r == cz - 1, jnp.where(second, 1.0, -1.0),
                  jnp.where((r == cz) & second, -2.0, 0.0)),
    ).astype(jnp.bfloat16)

    def landing(step, side):
        return halo.at[side, :, rows, :] if step == 0 else arrived.at[step - 1, side]

    def halo_copy(step, side):
        if step == 0:
            src = now_hbm.at[:, 0 if side == 0 else width - 1]
        else:
            src = sendbuf.at[step - 1, side]
        return pltpu.make_async_remote_copy(
            src_ref=src,
            dst_ref=landing(step, 1 - side),
            send_sem=hs_sems.at[step, side],
            recv_sem=hr_sems.at[step, 1 - side],
            device_id={"gx": me - 1 if side == 0 else me + 1},
            device_id_type=pl.DeviceIdType.MESH,
        )

    def halo_arrived(step, side):
        return pltpu.make_async_remote_copy(
            src_ref=landing(step, side),
            dst_ref=landing(step, side),
            send_sem=hs_sems.at[step, side],
            recv_sem=hr_sems.at[step, side],
            device_id={"gx": me - 1 if side == 0 else me + 1},
            device_id_type=pl.DeviceIdType.MESH,
        )

    def send_halo(step):
        for side, has in ((0, has_low), (1, has_high)):
            @pl.when(has)
            def _(side=side):
                halo_copy(step, side).start()

    def z_terms(p):
        return jnp.dot(p.astype(jnp.bfloat16), zmat[...], preferred_element_type=F32)

    def prepare(x, carry):
        found = z_terms(buf0[:, x, rows, :].reshape(2 * ny, nz))
        theta_s, theta_c = sin_cos(tilt[x].astype(F32))
        alpha_s, alpha_c = sin_cos(azi[x].astype(F32))
        speed = cou[x].astype(F32)
        e2 = eps[x].astype(F32) * 2.0
        scaled = speed * e2
        base = speed + scaled
        nx = theta_s * alpha_c
        nyy = theta_s * alpha_s
        sx = scaled * nx
        sy = scaled * nyy
        scz = scaled * theta_c
        mxx = base - sx * nx
        myy = base - sy * nyy
        coef[0, x] = mxx
        coef[1, x] = myy
        coef[2, x] = base - scz * theta_c
        coef[3, x] = -0.5 * (sx * nyy)
        coef[4, x] = -0.5 * (scz * nx)
        coef[5, x] = -0.5 * (scz * nyy)
        coef[6, x] = 2.0 - 2.0 * (mxx + myy)
        sz0[:, x, rows, :] = found[:, :nz].reshape(2, ny, nz)
        dz0[:, x, rows, :] = found[:, nz:].reshape(2, ny, nz)
        return carry

    for g in range(GROUPS):
        for copy in group_copies(g):
            copy.wait()
        lax.fori_loop(g * group, (g + 1) * group, prepare, 0, unroll=4)
        if g == 0:
            pl.semaphore_wait(barrier, n - 1)
            send_halo(0)
    prev_copy.wait()

    def combine(cs, p, old, px, sy, sz, yx, dzx, dzy):
        acc = cs[6] * p - old
        acc += cs[0] * px + cs[1] * sy
        acc += cs[2] * sz + cs[3] * yx
        acc += cs[4] * dzx + cs[5] * dzy
        return acc

    def edges(step):
        now, prv = bufs[step % 2], bufs[(step + 1) % 2]
        sz, dz = szs[step % 2], dzs[step % 2]
        for side, has in ((0, has_low), (1, has_high)):
            @pl.when(has)
            def _(side=side):
                halo_arrived(step, side).wait_recv()
        if step == 0:
            both = halo[:, :, rows, :].reshape(4 * ny, nz).astype(jnp.bfloat16)
        else:
            both = arrived[step - 1].reshape(4 * ny, nz)
        outer = jnp.dot(both, zmat[:, nz:], preferred_element_type=F32)
        if step > 0:
            halo[:, :, rows, :] = arrived[step - 1].astype(F32)
        for side in range(2):
            x = 0 if side == 0 else width - 1
            inner = 1 if side == 0 else width - 2
            for y in range(0, ny, EDGE):
                mid, up, dn = [pl.ds(PAD + y + d, EDGE) for d in (0, 1, -1)]
                cs = [coef[k, x, pl.ds(y, EDGE), :] for k in range(7)]
                for f in range(2):
                    a = halo[side, f, mid, :]
                    ya = halo[side, f, up, :] - halo[side, f, dn, :]
                    first = (side * 2 + f) * ny + y
                    za = outer[first : first + EDGE]
                    b = now[f, inner, mid, :]
                    yb = now[f, inner, up, :] - now[f, inner, dn, :]
                    zb = dz[f, inner, mid, :]
                    acc = combine(
                        cs, now[f, x, mid, :], prv[f, x, mid, :], a + b,
                        now[f, x, up, :] + now[f, x, dn, :], sz[f, x, mid, :],
                        yb - ya if side == 0 else ya - yb,
                        zb - za if side == 0 else za - zb,
                        dz[f, x, up, :] - dz[f, x, dn, :],
                    )
                    prv[f, x, mid, :] = acc
                    if step < STEPS - 1:
                        sendbuf[step, side, f, pl.ds(y, EDGE), :] = acc.astype(SEND)
        if step < STEPS - 1:
            send_halo(step + 1)

    def inside(step, base, emit, tall):
        now, prv = bufs[step % 2], bufs[(step + 1) % 2]
        sz, dz = szs[step % 2], dzs[step % 2]
        mid, up, dn = [pl.ds(base + PAD + d, tall) for d in (0, 1, -1)]
        here = pl.ds(base, tall)
        p0, y0, d0, p1, y1, s1, d1 = [[None, None] for _ in range(7)]
        for f in range(2):
            p0[f] = now[f, 0, mid, :]
            y0[f] = now[f, 0, up, :] - now[f, 0, dn, :]
            d0[f] = dz[f, 0, mid, :]
            hi, lo = now[f, 1, up, :], now[f, 1, dn, :]
            p1[f], y1[f], s1[f], d1[f] = now[f, 1, mid, :], hi - lo, hi + lo, dz[f, 1, mid, :]
        for x in range(1, width - 1):
            cs = [coef[k, x, here, :] for k in range(7)]
            for f in range(2):
                hi, lo = now[f, x + 1, up, :], now[f, x + 1, dn, :]
                p2, y2, s2, d2 = now[f, x + 1, mid, :], hi - lo, hi + lo, dz[f, x + 1, mid, :]
                acc = combine(
                    cs, p1[f], prv[f, x, mid, :], p2 + p0[f], s1[f], sz[f, x, mid, :],
                    y2 - y0[f], d2 - d0[f], dz[f, x, up, :] - dz[f, x, dn, :],
                )
                emit(f, x, mid, acc)
                p0[f], y0[f], d0[f] = p1[f], y1[f], d1[f]
                p1[f], y1[f], s1[f], d1[f] = p2, y2, s2, d2

    def z_rows(step, base):
        prv, sz, dz = bufs[(step + 1) % 2], szs[(step + 1) % 2], dzs[(step + 1) % 2]
        at = pl.ds(base, TALL)
        found = z_terms(jnp.concatenate([prv[f, x, at, :] for x in range(width) for f in range(2)], axis=0))
        for x in range(width):
            for f in range(2):
                first = (x * 2 + f) * TALL
                sz[f, x, at, :] = found[first : first + TALL, :nz]
                dz[f, x, at, :] = found[first : first + TALL, nz:]

    for step in range(STEPS - 1):
        edges(step)

        def emit(f, x, mid, acc, prv=bufs[(step + 1) % 2]):
            prv[f, x, mid, :] = acc

        def advance(k, carry, step=step, emit=emit):
            base = pl.multiple_of(k * TALL, TALL)
            z_rows(step, base + PAD - TALL)
            inside(step, base, emit, TALL)
            return carry

        lax.fori_loop(0, ny // TALL, advance, 0)
        z_rows(step, PAD + ny - TALL)

    edges(STEPS - 1)
    final = bufs[STEPS % 2]
    span = jr * half
    each = n // chunks

    def piece(target, source):
        start = pl.multiple_of(((target * cols_per) // nz) * half, half)
        return pltpu.make_async_remote_copy(
            src_ref=snap_send.at[:, pl.ds(start, span), :],
            dst_ref=cols_ref.at[source],
            send_sem=as_sems.at[target],
            recv_sem=ar_sems.at[source],
            device_id={"gx": target},
            device_id_type=pl.DeviceIdType.MESH,
        )

    start = pl.multiple_of(((me * cols_per) // nz) * half, half)
    own = pltpu.make_async_copy(snap_send.at[:, pl.ds(start, span), :], cols_ref.at[me], own_sem)

    def last(k, carry):
        mine = me // each
        low = 2 * mine < chunks
        near = jnp.where(low, mine, chunks - 1 - mine)
        lead = chunks - 1 - 2 * near
        rest = jnp.maximum(k - lead, 0)
        pick = jnp.where(lax.rem(rest, 2) == 0, 2 * near - rest // 2, rest // 2)
        pick = jnp.where(k < lead, chunks - 1 - k, pick)
        block = jnp.where(low, pick, chunks - 1 - pick)
        base = pl.multiple_of(block * ROWS, ROWS)
        mid = pl.ds(base + PAD, ROWS)
        held = [final[f, 0, mid, :] for f in range(2)]

        def emit(f, x, mid, acc):
            if x % 2 == 0:
                held[f] = acc
            else:
                pair[f, pl.ds((x // 2) * ROWS, ROWS), :] = held[f] + acc

        inside(STEPS - 1, base, emit, ROWS)
        for f in range(2):
            pair[f, pl.ds((half - 1) * ROWS, ROWS), :] = held[f] + final[f, width - 1, mid, :]
        for f in range(2):
            for j in range(ROWS // 2):
                even = pair[f, pl.ds(2 * j, half, stride=ROWS), :]
                odd = pair[f, pl.ds(2 * j + 1, half, stride=ROWS), :]
                at = pl.multiple_of((block * (ROWS // 2) + j) * half, half)
                snap_send[f, pl.ds(at, half), :] = ((even + odd) * 0.25).astype(SEND)

        def send(u, carry):
            target = block * each + u

            @pl.when(target != me)
            def _():
                piece(target, me).start()

            return carry

        lax.fori_loop(0, each, send, 0)
        return carry

    lax.fori_loop(0, chunks, last, 0)
    own.start()

    for step in range(STEPS):
        for side, has in ((0, has_low), (1, has_high)):
            @pl.when(has)
            def _(step=step, side=side):
                halo_copy(step, side).wait_send()

    def wait_piece(k, carry):
        piece(lax.rem(me + k, n), me).wait_send()
        piece(lax.rem(me + k, n), lax.rem(me + k, n)).wait_recv()
        return carry

    lax.fori_loop(1, n, wait_piece, 0)
    own.wait()


def image_kernel(
    cols_per, jr, offsets, tables_at, cols_ref, tab_ref, out_ref, lines, wide, keep, *prods
):
    n = cols_ref.shape[0]
    half = cols_ref.shape[2] // jr
    nz = cols_ref.shape[3]
    full = n * half
    step = pl.program_id(0)
    tables = tab_ref.shape[0]
    angles = tab_ref.shape[1]
    lags = tab_ref.shape[2]

    @pl.when(step == 0)
    def _():
        for f in range(2):
            for j in range(jr):
                for t in range(full // nz):
                    per = nz // half
                    block = cols_ref[pl.ds(t * per, per), f, pl.ds(j * half, half), :]
                    block = block.reshape(nz, nz).astype(F32)
                    lines[f, j, :, pl.ds(t * nz, nz)] = block.T.astype(SEND)
        lag = lax.broadcasted_iota(jnp.int32, (lags, lags * 8), 0)
        col = lax.broadcasted_iota(jnp.int32, (lags, lags * 8), 1)
        spread = jnp.where(col // 8 == lag, 1.0, 0.0).astype(jnp.bfloat16)
        flat = tab_ref[...].reshape(tables * angles, lags)
        wide[...] = jnp.dot(flat, spread, preferred_element_type=F32).astype(jnp.bfloat16)
        row_c = lax.rem(lax.broadcasted_iota(jnp.int32, (angles * 8, lags * 8), 0), 8)
        col_c = lax.rem(lax.broadcasted_iota(jnp.int32, (angles * 8, lags * 8), 1), 8)
        keep[...] = jnp.where(row_c == col_c, 1.0, 0.0).astype(jnp.bfloat16)

    me = lax.axis_index("gx")
    z0 = lax.rem(me * cols_per, nz)
    tiles = full // nz
    ta = tables * angles

    sub = lax.broadcasted_iota(jnp.int32, (8, ta), 0)
    lane_ta = lax.broadcasted_iota(jnp.int32, (angles, 8, ta), 2)
    row_a = lax.broadcasted_iota(jnp.int32, (angles, 8, ta), 0)
    weights = []
    for q in range(DEPTH // 8):
        row0 = z0 + step * DEPTH + q * 8
        chosen = jnp.zeros((8, ta), jnp.int32)
        for c in range(8):
            chosen = jnp.where(sub == c, tables_at[row0 + c], chosen)
        wanted = (chosen * angles)[None] + row_a
        pick = jnp.where(lane_ta == wanted, 1.0, 0.0).reshape(angles * 8, ta)
        dense = jnp.dot(pick.astype(jnp.bfloat16), wide[...], preferred_element_type=F32)
        weights.append(dense.astype(jnp.bfloat16) * keep[...])

    lane = lax.broadcasted_iota(jnp.int16, (DEPTH, nz), 1)
    zero = jnp.zeros((DEPTH, nz), SEND)

    def moved(parts, d):
        if d == 0:
            return parts
        turned = [pltpu.roll(part, d % nz, axis=1) for part in parts]
        if d > 0:
            return [
                jnp.where(lane >= d, turned[t], turned[t - 1] if t else zero)
                for t in range(tiles)
            ]
        return [
            jnp.where(lane < nz + d, turned[t], turned[t + 1] if t + 1 < tiles else zero)
            for t in range(tiles)
        ]

    row0 = pl.multiple_of(z0 + step * DEPTH, DEPTH)
    for j in range(jr):
        source = [lines[0, j, pl.ds(row0, DEPTH), pl.ds(t * nz, nz)] for t in range(tiles)]
        receiver = [lines[1, j, pl.ds(row0, DEPTH), pl.ds(t * nz, nz)] for t in range(tiles)]
        for d in range(-LAG_REACH, LAG_REACH):
            left, right = moved(source, d), moved(receiver, -d)
            for t in range(tiles):
                product = (left[t] * right[t]).astype(F32)
                for q in range(DEPTH // 8):
                    prods[j * (DEPTH // 8) + q][d + LAG_REACH, :, pl.ds(t * nz, nz)] = product[8 * q : 8 * q + 8]

    for j in range(jr):
        results = []
        for q in range(DEPTH // 8):
            lagged = jnp.concatenate(
                [prods[j * (DEPTH // 8) + q][offsets[h] + LAG_REACH] for h in range(lags)], axis=0
            ).astype(jnp.bfloat16)
            total = jnp.dot(weights[q], lagged, preferred_element_type=F32)
            results.append(total.reshape(angles, 8, full))
        out_ref[:, j] = jnp.concatenate(results, axis=1).astype(jnp.bfloat16)


def local(
    waves_now, waves_prev, epsilon, tilt, azimuth, courant, lag_offsets, table_index, lag_tables
):
    n = lax.axis_size("gx")
    width, ny, nz = epsilon.shape
    half = width // 2
    columns = (ny // 2) * nz
    cols_per = columns // n
    jr = max(1, cols_per // nz)
    full = n * half
    plane = (2, width, ny + 2 * PAD, nz)
    dma = pltpu.SemaphoreType.DMA
    cols = pl.pallas_call(
        functools.partial(wave_kernel, n, jr, cols_per),
        out_shape=jax.ShapeDtypeStruct((n, 2, jr * half, nz), SEND),
        in_specs=[pl.BlockSpec(memory_space=pltpu.HBM)] * 6,
        out_specs=pl.BlockSpec(memory_space=pl.ANY),
        scratch_shapes=[
            pltpu.VMEM(plane, F32),
            pltpu.VMEM(plane, F32),
            pltpu.VMEM(plane, F32),
            pltpu.VMEM(plane, F32),
            pltpu.VMEM(plane, F32),
            pltpu.VMEM(plane, F32),
            pltpu.VMEM((width, ny, nz), epsilon.dtype),
            pltpu.VMEM((width, ny, nz), tilt.dtype),
            pltpu.VMEM((width, ny, nz), azimuth.dtype),
            pltpu.VMEM((width, ny, nz), courant.dtype),
            pltpu.VMEM((7, width, ny, nz), F32),
            pltpu.VMEM((nz, 2 * nz), jnp.bfloat16),
            pltpu.VMEM((2, half * ROWS, nz), F32),
            pltpu.VMEM((2, (ny // 2) * half, nz), SEND),
            pltpu.VMEM((STEPS - 1, 2, 2, ny, nz), SEND),
            pltpu.VMEM((2, 2, ny + 2 * PAD, nz), F32),
            pltpu.VMEM((STEPS - 1, 2, 2, ny, nz), SEND),
            dma((GROUPS, 5)),
            dma,
            dma,
            dma((STEPS, 2)),
            dma((STEPS, 2)),
            dma((n,)),
            dma((n,)),
        ],
        compiler_params=pltpu.CompilerParams(
            collective_id=0, has_side_effects=True, vmem_limit_bytes=60 << 20
        ),
        name="waves",
    )(waves_now, waves_prev, epsilon, tilt, azimuth, courant)

    angles, lags = lag_tables.shape[1:]
    tables = lag_tables.shape[0]
    cz = min(cols_per, nz)
    image = pl.pallas_call(
        functools.partial(image_kernel, cols_per, jr),
        grid=(cz // DEPTH,),
        out_shape=jax.ShapeDtypeStruct((angles, jr, cz, full), jnp.bfloat16),
        in_specs=[
            pl.BlockSpec(memory_space=pltpu.SMEM),
            pl.BlockSpec(memory_space=pltpu.SMEM),
            pl.BlockSpec(memory_space=pltpu.VMEM),
            pl.BlockSpec(memory_space=pltpu.VMEM),
        ],
        out_specs=pl.BlockSpec((angles, jr, DEPTH, full), lambda g: (0, 0, g, 0)),
        scratch_shapes=[
            pltpu.VMEM((2, jr, nz, full), SEND),
            pltpu.VMEM((tables * angles, lags * 8), jnp.bfloat16),
            pltpu.VMEM((angles * 8, lags * 8), jnp.bfloat16),
        ] + [pltpu.VMEM((2 * LAG_REACH, 8, full), F32)] * (jr * (DEPTH // 8)),
        compiler_params=pltpu.CompilerParams(vmem_limit_bytes=60 << 20),
        name="image",
    )(lag_offsets, table_index, cols, lag_tables)
    return image.reshape(angles, cols_per, full)


def solution(mesh):
    wave = P(None, ("shot", "gx"), None, None)
    cell = P("gx", None, None)
    return jax.shard_map(
        local,
        mesh=mesh,
        in_specs=(wave, wave, cell, cell, cell, cell, P(), P(), P()),
        out_specs=P(None, ("shot", "gx"), None),
        check_vma=False,
    )
```

```python
import functools
import jax
import jax.numpy as jnp
from jax import lax
from jax.experimental import pallas as pl
from jax.experimental.pallas import tpu as pltpu
from jax.sharding import PartitionSpec as P

STEPS = 4
LAG_REACH = 16
PAD = 16
ROWS = 8
DEPTH = 64
TALL = 16
EDGE = 32
GROUPS = 4
F32 = jnp.float32
SEND = jnp.bfloat16


def sin_cos(x):
    u = x * x
    s = u * 7.206469580499954e-09 - 2.1888434293738905e-06
    s = s * u + 0.00036827396667825314
    s = s * u - 0.029462771608356236
    s = s * u + 0.7071067811865476
    s = s * x
    c = u * -3.6015480241538463e-10 + 1.3679165339017438e-07
    c = c * u - 3.0689327892292986e-05
    c = c * u + 0.003682845531587343
    c = c * u - 0.17677669370892954
    c = c * u + 1.4142135623730951
    return s * c, 1.0 - s * s


def wave_kernel(
    n, jr, cols_per, now_hbm, prev_hbm, eps_hbm, tilt_hbm, azi_hbm, cou_hbm, cols_ref,
    buf0, buf1, sz0, sz1, dz0, dz1, eps, tilt, azi, cou, coef, zmat, pair, snap_send, sendbuf, halo, arrived,
    in_sems, prev_sem, own_sem, hs_sems, hr_sems, as_sems, ar_sems,
):
    width = eps.shape[0]
    ny = eps.shape[1]
    nz = eps.shape[2]
    half = width // 2
    chunks = ny // ROWS
    rows = pl.ds(PAD, ny)
    me = lax.axis_index("gx")
    has_low = me > 0
    has_high = me < n - 1
    bufs = (buf0, buf1)
    szs = (sz0, sz1)
    dzs = (dz0, dz1)
    group = width // GROUPS

    def group_copies(g):
        part = pl.ds(g * group, group)
        pairs = (
            (tilt_hbm.at[part], tilt.at[part]),
            (azi_hbm.at[part], azi.at[part]),
            (eps_hbm.at[part], eps.at[part]),
            (cou_hbm.at[part], cou.at[part]),
            (now_hbm.at[:, part], buf0.at[:, part, rows, :]),
        )
        return [
            pltpu.make_async_copy(src, dst, in_sems.at[g, k]) for k, (src, dst) in enumerate(pairs)
        ]

    for g in range(GROUPS):
        for copy in group_copies(g):
            copy.start()
    prev_copy = pltpu.make_async_copy(prev_hbm, buf1.at[:, :, rows, :], prev_sem)
    prev_copy.start()

    barrier = pltpu.get_barrier_semaphore()

    def greet(k, carry):
        pl.semaphore_signal(
            barrier, inc=1, device_id={"gx": lax.rem(me + k, n)},
            device_id_type=pl.DeviceIdType.MESH,
        )
        return carry

    lax.fori_loop(1, n, greet, 0)

    zero_rows = jnp.zeros((2, width, PAD, nz), F32)
    for ref in (buf0, buf1, dz0, dz1):
        ref[:, :, pl.ds(0, PAD), :] = zero_rows
        ref[:, :, pl.ds(PAD + ny, PAD), :] = zero_rows
    zero_ends = jnp.zeros((2, 2, PAD, nz), F32)
    halo[:, :, pl.ds(0, PAD), :] = zero_ends
    halo[:, :, pl.ds(PAD + ny, PAD), :] = zero_ends
    for side, has in ((0, has_low), (1, has_high)):
        @pl.when(jnp.logical_not(has))
        def _(side=side):
            halo[side, :, rows, :] = jnp.zeros((2, ny, nz), F32)
            arrived[:, side] = jnp.zeros((STEPS - 1, 2, ny, nz), SEND)

    r = lax.broadcasted_iota(jnp.int32, (nz, 2 * nz), 0)
    c = lax.broadcasted_iota(jnp.int32, (nz, 2 * nz), 1)
    second = c < nz
    cz = jnp.where(second, c, c - nz)
    zmat[...] = jnp.where(
        r == cz + 1, 1.0,
        jnp.where(r == cz - 1, jnp.where(second, 1.0, -1.0),
                  jnp.where((r == cz) & second, -2.0, 0.0)),
    ).astype(jnp.bfloat16)

    def landing(step, side):
        return halo.at[side, :, rows, :] if step == 0 else arrived.at[step - 1, side]

    def halo_copy(step, side):
        if step == 0:
            src = now_hbm.at[:, 0 if side == 0 else width - 1]
        else:
            src = sendbuf.at[step - 1, side]
        return pltpu.make_async_remote_copy(
            src_ref=src,
            dst_ref=landing(step, 1 - side),
            send_sem=hs_sems.at[step, side],
            recv_sem=hr_sems.at[step, 1 - side],
            device_id={"gx": me - 1 if side == 0 else me + 1},
            device_id_type=pl.DeviceIdType.MESH,
        )

    def halo_arrived(step, side):
        return pltpu.make_async_remote_copy(
            src_ref=landing(step, side),
            dst_ref=landing(step, side),
            send_sem=hs_sems.at[step, side],
            recv_sem=hr_sems.at[step, side],
            device_id={"gx": me - 1 if side == 0 else me + 1},
            device_id_type=pl.DeviceIdType.MESH,
        )

    def send_halo(step):
        for side, has in ((0, has_low), (1, has_high)):
            @pl.when(has)
            def _(side=side):
                halo_copy(step, side).start()

    def z_terms(p):
        return jnp.dot(p.astype(jnp.bfloat16), zmat[...], preferred_element_type=F32)

    def prepare(x, carry):
        found = z_terms(buf0[:, x, rows, :].reshape(2 * ny, nz))
        theta_s, theta_c = sin_cos(tilt[x].astype(F32))
        alpha_s, alpha_c = sin_cos(azi[x].astype(F32))
        speed = cou[x].astype(F32)
        e2 = eps[x].astype(F32) * 2.0
        scaled = speed * e2
        base = speed + scaled
        nx = theta_s * alpha_c
        nyy = theta_s * alpha_s
        sx = scaled * nx
        sy = scaled * nyy
        scz = scaled * theta_c
        mxx = base - sx * nx
        myy = base - sy * nyy
        coef[0, x] = mxx
        coef[1, x] = myy
        coef[2, x] = base - scz * theta_c
        coef[3, x] = -0.5 * (sx * nyy)
        coef[4, x] = -0.5 * (scz * nx)
        coef[5, x] = -0.5 * (scz * nyy)
        coef[6, x] = 2.0 - 2.0 * (mxx + myy)
        sz0[:, x, rows, :] = found[:, :nz].reshape(2, ny, nz)
        dz0[:, x, rows, :] = found[:, nz:].reshape(2, ny, nz)
        return carry

    for g in range(GROUPS):
        for copy in group_copies(g):
            copy.wait()
        lax.fori_loop(g * group, (g + 1) * group, prepare, 0, unroll=4)
        if g == 0:
            pl.semaphore_wait(barrier, n - 1)
            send_halo(0)
    prev_copy.wait()

    def combine(cs, p, old, px, sy, sz, yx, dzx, dzy):
        acc = cs[6] * p - old
        acc += cs[0] * px + cs[1] * sy
        acc += cs[2] * sz + cs[3] * yx
        acc += cs[4] * dzx + cs[5] * dzy
        return acc

    def edges(step):
        now, prv = bufs[step % 2], bufs[(step + 1) % 2]
        sz, dz = szs[step % 2], dzs[step % 2]
        for side, has in ((0, has_low), (1, has_high)):
            @pl.when(has)
            def _(side=side):
                halo_arrived(step, side).wait_recv()
        if step == 0:
            both = halo[:, :, rows, :].reshape(4 * ny, nz).astype(jnp.bfloat16)
        else:
            both = arrived[step - 1].reshape(4 * ny, nz)
        outer = jnp.dot(both, zmat[:, nz:], preferred_element_type=F32)
        if step > 0:
            halo[:, :, rows, :] = arrived[step - 1].astype(F32)
        for side in range(2):
            x = 0 if side == 0 else width - 1
            inner = 1 if side == 0 else width - 2
            for y in range(0, ny, EDGE):
                mid, up, dn = [pl.ds(PAD + y + d, EDGE) for d in (0, 1, -1)]
                cs = [coef[k, x, pl.ds(y, EDGE), :] for k in range(7)]
                for f in range(2):
                    a = halo[side, f, mid, :]
                    ya = halo[side, f, up, :] - halo[side, f, dn, :]
                    first = (side * 2 + f) * ny + y
                    za = outer[first : first + EDGE]
                    b = now[f, inner, mid, :]
                    yb = now[f, inner, up, :] - now[f, inner, dn, :]
                    zb = dz[f, inner, mid, :]
                    acc = combine(
                        cs, now[f, x, mid, :], prv[f, x, mid, :], a + b,
                        now[f, x, up, :] + now[f, x, dn, :], sz[f, x, mid, :],
                        yb - ya if side == 0 else ya - yb,
                        zb - za if side == 0 else za - zb,
                        dz[f, x, up, :] - dz[f, x, dn, :],
                    )
                    prv[f, x, mid, :] = acc
                    if step < STEPS - 1:
                        sendbuf[step, side, f, pl.ds(y, EDGE), :] = acc.astype(SEND)
        if step < STEPS - 1:
            send_halo(step + 1)

    def inside(step, base, emit, tall):
        now, prv = bufs[step % 2], bufs[(step + 1) % 2]
        sz, dz = szs[step % 2], dzs[step % 2]
        mid, up, dn = [pl.ds(base + PAD + d, tall) for d in (0, 1, -1)]
        here = pl.ds(base, tall)
        p0, y0, d0, p1, y1, s1, d1 = [[None, None] for _ in range(7)]
        for f in range(2):
            p0[f] = now[f, 0, mid, :]
            y0[f] = now[f, 0, up, :] - now[f, 0, dn, :]
            d0[f] = dz[f, 0, mid, :]
            hi, lo = now[f, 1, up, :], now[f, 1, dn, :]
            p1[f], y1[f], s1[f], d1[f] = now[f, 1, mid, :], hi - lo, hi + lo, dz[f, 1, mid, :]
        for x in range(1, width - 1):
            cs = [coef[k, x, here, :] for k in range(7)]
            for f in range(2):
                hi, lo = now[f, x + 1, up, :], now[f, x + 1, dn, :]
                p2, y2, s2, d2 = now[f, x + 1, mid, :], hi - lo, hi + lo, dz[f, x + 1, mid, :]
                acc = combine(
                    cs, p1[f], prv[f, x, mid, :], p2 + p0[f], s1[f], sz[f, x, mid, :],
                    y2 - y0[f], d2 - d0[f], dz[f, x, up, :] - dz[f, x, dn, :],
                )
                emit(f, x, mid, acc)
                p0[f], y0[f], d0[f] = p1[f], y1[f], d1[f]
                p1[f], y1[f], s1[f], d1[f] = p2, y2, s2, d2

    def z_rows(step, base):
        prv, sz, dz = bufs[(step + 1) % 2], szs[(step + 1) % 2], dzs[(step + 1) % 2]
        at = pl.ds(base, TALL)
        found = z_terms(jnp.concatenate([prv[f, x, at, :] for x in range(width) for f in range(2)], axis=0))
        for x in range(width):
            for f in range(2):
                first = (x * 2 + f) * TALL
                sz[f, x, at, :] = found[first : first + TALL, :nz]
                dz[f, x, at, :] = found[first : first + TALL, nz:]

    for step in range(STEPS - 1):
        edges(step)

        def emit(f, x, mid, acc, prv=bufs[(step + 1) % 2]):
            prv[f, x, mid, :] = acc

        def advance(k, carry, step=step, emit=emit):
            base = pl.multiple_of(k * TALL, TALL)
            z_rows(step, base + PAD - TALL)
            inside(step, base, emit, TALL)
            return carry

        lax.fori_loop(0, ny // TALL, advance, 0)
        z_rows(step, PAD + ny - TALL)

    edges(STEPS - 1)
    final = bufs[STEPS % 2]
    span = jr * half
    each = n // chunks

    def piece(target, source):
        start = pl.multiple_of(((target * cols_per) // nz) * half, half)
        return pltpu.make_async_remote_copy(
            src_ref=snap_send.at[:, pl.ds(start, span), :],
            dst_ref=cols_ref.at[source],
            send_sem=as_sems.at[target],
            recv_sem=ar_sems.at[source],
            device_id={"gx": target},
            device_id_type=pl.DeviceIdType.MESH,
        )

    start = pl.multiple_of(((me * cols_per) // nz) * half, half)
    own = pltpu.make_async_copy(snap_send.at[:, pl.ds(start, span), :], cols_ref.at[me], own_sem)

    def last(k, carry):
        mine = me // each
        low = 2 * mine < chunks
        near = jnp.where(low, mine, chunks - 1 - mine)
        lead = chunks - 1 - 2 * near
        rest = jnp.maximum(k - lead, 0)
        pick = jnp.where(lax.rem(rest, 2) == 0, 2 * near - rest // 2, rest // 2)
        pick = jnp.where(k < lead, chunks - 1 - k, pick)
        block = jnp.where(low, pick, chunks - 1 - pick)
        base = pl.multiple_of(block * ROWS, ROWS)
        mid = pl.ds(base + PAD, ROWS)
        held = [final[f, 0, mid, :] for f in range(2)]

        def emit(f, x, mid, acc):
            if x % 2 == 0:
                held[f] = acc
            else:
                pair[f, pl.ds((x // 2) * ROWS, ROWS), :] = held[f] + acc

        inside(STEPS - 1, base, emit, ROWS)
        for f in range(2):
            pair[f, pl.ds((half - 1) * ROWS, ROWS), :] = held[f] + final[f, width - 1, mid, :]
        for f in range(2):
            for j in range(ROWS // 2):
                even = pair[f, pl.ds(2 * j, half, stride=ROWS), :]
                odd = pair[f, pl.ds(2 * j + 1, half, stride=ROWS), :]
                at = pl.multiple_of((block * (ROWS // 2) + j) * half, half)
                snap_send[f, pl.ds(at, half), :] = ((even + odd) * 0.25).astype(SEND)

        def send(u, carry):
            target = block * each + u

            @pl.when(target != me)
            def _():
                piece(target, me).start()

            return carry

        lax.fori_loop(0, each, send, 0)
        return carry

    lax.fori_loop(0, chunks, last, 0)
    own.start()

    for step in range(STEPS):
        for side, has in ((0, has_low), (1, has_high)):
            @pl.when(has)
            def _(step=step, side=side):
                halo_copy(step, side).wait_send()

    def wait_piece(k, carry):
        piece(lax.rem(me + k, n), me).wait_send()
        piece(lax.rem(me + k, n), lax.rem(me + k, n)).wait_recv()
        return carry

    lax.fori_loop(1, n, wait_piece, 0)
    own.wait()


def image_kernel(
    cols_per, jr, depth, offsets, tables_at, cols_ref, tab_ref, out_ref, lines, wide, keep, *prods
):
    n = cols_ref.shape[0]
    half = cols_ref.shape[2] // jr
    nz = cols_ref.shape[3]
    full = n * half
    step = pl.program_id(0)
    tables = tab_ref.shape[0]
    angles = tab_ref.shape[1]
    lags = tab_ref.shape[2]

    @pl.when(step == 0)
    def _():
        for f in range(2):
            for j in range(jr):
                for t in range(full // nz):
                    per = nz // half
                    block = cols_ref[pl.ds(t * per, per), f, pl.ds(j * half, half), :]
                    block = block.reshape(nz, nz).astype(F32)
                    lines[f, j, :, pl.ds(t * nz, nz)] = block.T.astype(SEND)
        lag = lax.broadcasted_iota(jnp.int32, (lags, lags * 8), 0)
        col = lax.broadcasted_iota(jnp.int32, (lags, lags * 8), 1)
        spread = jnp.where(col // 8 == lag, 1.0, 0.0).astype(jnp.bfloat16)
        flat = tab_ref[...].reshape(tables * angles, lags)
        wide[...] = jnp.dot(flat, spread, preferred_element_type=F32).astype(jnp.bfloat16)
        row_c = lax.rem(lax.broadcasted_iota(jnp.int32, (angles * 8, lags * 8), 0), 8)
        col_c = lax.rem(lax.broadcasted_iota(jnp.int32, (angles * 8, lags * 8), 1), 8)
        keep[...] = jnp.where(row_c == col_c, 1.0, 0.0).astype(jnp.bfloat16)

    me = lax.axis_index("gx")
    z0 = lax.rem(me * cols_per, nz)
    tiles = full // nz
    ta = tables * angles

    lane = lax.broadcasted_iota(jnp.int16, (depth, nz), 1)
    zero = jnp.zeros((depth, nz), SEND)

    def moved(parts, d):
        if d == 0:
            return parts
        turned = [pltpu.roll(part, d % nz, axis=1) for part in parts]
        if d > 0:
            return [
                jnp.where(lane >= d, turned[t], turned[t - 1] if t else zero)
                for t in range(tiles)
            ]
        return [
            jnp.where(lane < nz + d, turned[t], turned[t + 1] if t + 1 < tiles else zero)
            for t in range(tiles)
        ]

    row0 = pl.multiple_of(z0 + step * depth, depth)
    for j in range(jr):
        source = [lines[0, j, pl.ds(row0, depth), pl.ds(t * nz, nz)] for t in range(tiles)]
        receiver = [lines[1, j, pl.ds(row0, depth), pl.ds(t * nz, nz)] for t in range(tiles)]
        for d in range(-LAG_REACH, LAG_REACH):
            left, right = moved(source, d), moved(receiver, -d)
            for t in range(tiles):
                product = (left[t] * right[t]).astype(F32)
                for q in range(depth // 8):
                    prods[j * (depth // 8) + q][d + LAG_REACH, :, pl.ds(t * nz, nz)] = product[8 * q : 8 * q + 8]

    sub = lax.broadcasted_iota(jnp.int32, (8, ta), 0)
    lane_ta = lax.broadcasted_iota(jnp.int32, (angles, 8, ta), 2)
    row_a = lax.broadcasted_iota(jnp.int32, (angles, 8, ta), 0)
    weights = []
    for q in range(depth // 8):
        row0 = z0 + step * depth + q * 8
        chosen = jnp.zeros((8, ta), jnp.int32)
        for c in range(8):
            chosen = jnp.where(sub == c, tables_at[row0 + c], chosen)
        wanted = (chosen * angles)[None] + row_a
        pick = jnp.where(lane_ta == wanted, 1.0, 0.0).reshape(angles * 8, ta)
        dense = jnp.dot(pick.astype(jnp.bfloat16), wide[...], preferred_element_type=F32)
        weights.append(dense.astype(jnp.bfloat16) * keep[...])

    for j in range(jr):
        results = []
        for q in range(depth // 8):
            lagged = jnp.concatenate(
                [prods[j * (depth // 8) + q][offsets[h] + LAG_REACH] for h in range(lags)], axis=0
            ).astype(jnp.bfloat16)
            total = jnp.dot(weights[q], lagged, preferred_element_type=F32)
            results.append(total.reshape(angles, 8, full))
        out_ref[:, j] = jnp.concatenate(results, axis=1).astype(jnp.bfloat16)


def local(
    waves_now, waves_prev, epsilon, tilt, azimuth, courant, lag_offsets, table_index, lag_tables
):
    n = lax.axis_size("gx")
    width, ny, nz = epsilon.shape
    half = width // 2
    columns = (ny // 2) * nz
    cols_per = columns // n
    jr = max(1, cols_per // nz)
    full = n * half
    plane = (2, width, ny + 2 * PAD, nz)
    dma = pltpu.SemaphoreType.DMA
    cols = pl.pallas_call(
        functools.partial(wave_kernel, n, jr, cols_per),
        out_shape=jax.ShapeDtypeStruct((n, 2, jr * half, nz), SEND),
        in_specs=[pl.BlockSpec(memory_space=pltpu.HBM)] * 6,
        out_specs=pl.BlockSpec(memory_space=pl.ANY),
        scratch_shapes=[
            pltpu.VMEM(plane, F32),
            pltpu.VMEM(plane, F32),
            pltpu.VMEM(plane, F32),
            pltpu.VMEM(plane, F32),
            pltpu.VMEM(plane, F32),
            pltpu.VMEM(plane, F32),
            pltpu.VMEM((width, ny, nz), epsilon.dtype),
            pltpu.VMEM((width, ny, nz), tilt.dtype),
            pltpu.VMEM((width, ny, nz), azimuth.dtype),
            pltpu.VMEM((width, ny, nz), courant.dtype),
            pltpu.VMEM((7, width, ny, nz), F32),
            pltpu.VMEM((nz, 2 * nz), jnp.bfloat16),
            pltpu.VMEM((2, half * ROWS, nz), F32),
            pltpu.VMEM((2, (ny // 2) * half, nz), SEND),
            pltpu.VMEM((STEPS - 1, 2, 2, ny, nz), SEND),
            pltpu.VMEM((2, 2, ny + 2 * PAD, nz), F32),
            pltpu.VMEM((STEPS - 1, 2, 2, ny, nz), SEND),
            dma((GROUPS, 5)),
            dma,
            dma,
            dma((STEPS, 2)),
            dma((STEPS, 2)),
            dma((n,)),
            dma((n,)),
        ],
        compiler_params=pltpu.CompilerParams(
            collective_id=0, has_side_effects=True, vmem_limit_bytes=60 << 20
        ),
        name="waves",
    )(waves_now, waves_prev, epsilon, tilt, azimuth, courant)

    angles, lags = lag_tables.shape[1:]
    tables = lag_tables.shape[0]
    cz = min(cols_per, nz)
    depth = min(DEPTH, cz)
    image = pl.pallas_call(
        functools.partial(image_kernel, cols_per, jr, depth),
        grid=(cz // depth,),
        out_shape=jax.ShapeDtypeStruct((angles, jr, cz, full), jnp.bfloat16),
        in_specs=[
            pl.BlockSpec(memory_space=pltpu.SMEM),
            pl.BlockSpec(memory_space=pltpu.SMEM),
            pl.BlockSpec(memory_space=pltpu.VMEM),
            pl.BlockSpec(memory_space=pltpu.VMEM),
        ],
        out_specs=pl.BlockSpec((angles, jr, depth, full), lambda g: (0, 0, g, 0)),
        scratch_shapes=[
            pltpu.VMEM((2, jr, nz, full), SEND),
            pltpu.VMEM((tables * angles, lags * 8), jnp.bfloat16),
            pltpu.VMEM((angles * 8, lags * 8), jnp.bfloat16),
        ] + [pltpu.VMEM((2 * LAG_REACH, 8, full), F32)] * (jr * (depth // 8)),
        compiler_params=pltpu.CompilerParams(vmem_limit_bytes=60 << 20),
        name="image",
    )(lag_offsets, table_index, cols, lag_tables)
    return image.reshape(angles, cols_per, full)


def solution(mesh):
    wave = P(None, ("shot", "gx"), None, None)
    cell = P("gx", None, None)
    return jax.shard_map(
        local,
        mesh=mesh,
        in_specs=(wave, wave, cell, cell, cell, cell, P(), P(), P()),
        out_specs=P(None, ("shot", "gx"), None),
        check_vma=False,
    )
```

```python
import functools
import jax
import jax.numpy as jnp
from jax import lax
from jax.experimental import pallas as pl
from jax.experimental.pallas import tpu as pltpu
from jax.sharding import PartitionSpec as P

STEPS = 4
LAG_REACH = 16
PAD = 16
ROWS = 8
DEPTH = 64
TALL = 16
EDGE = 32
GROUPS = 4
F32 = jnp.float32
SEND = jnp.bfloat16


def sin_cos(x):
    u = x * x
    s = u * 7.206469580499954e-09 - 2.1888434293738905e-06
    s = s * u + 0.00036827396667825314
    s = s * u - 0.029462771608356236
    s = s * u + 0.7071067811865476
    s = s * x
    c = u * -3.6015480241538463e-10 + 1.3679165339017438e-07
    c = c * u - 3.0689327892292986e-05
    c = c * u + 0.003682845531587343
    c = c * u - 0.17677669370892954
    c = c * u + 1.4142135623730951
    return s * c, 1.0 - s * s


def wave_kernel(
    n, jr, cols_per, now_hbm, prev_hbm, eps_hbm, tilt_hbm, azi_hbm, cou_hbm, cols_ref,
    buf0, buf1, sz0, sz1, dz0, dz1, eps, tilt, azi, cou, coef, zmat, pair, snap_send, sendbuf, halo, arrived,
    in_sems, prev_sem, own_sem, hs_sems, hr_sems, as_sems, ar_sems,
):
    width = eps.shape[0]
    ny = eps.shape[1]
    nz = eps.shape[2]
    half = width // 2
    chunks = ny // ROWS
    rows = pl.ds(PAD, ny)
    me = lax.axis_index("gx")
    has_low = me > 0
    has_high = me < n - 1
    bufs = (buf0, buf1)
    szs = (sz0, sz1)
    dzs = (dz0, dz1)
    group = width // GROUPS

    def group_copies(g):
        part = pl.ds(g * group, group)
        pairs = (
            (tilt_hbm.at[part], tilt.at[part]),
            (azi_hbm.at[part], azi.at[part]),
            (eps_hbm.at[part], eps.at[part]),
            (cou_hbm.at[part], cou.at[part]),
            (now_hbm.at[:, part], buf0.at[:, part, rows, :]),
        )
        return [
            pltpu.make_async_copy(src, dst, in_sems.at[g, k]) for k, (src, dst) in enumerate(pairs)
        ]

    for g in range(GROUPS):
        for copy in group_copies(g):
            copy.start()
    prev_copy = pltpu.make_async_copy(prev_hbm, buf1.at[:, :, rows, :], prev_sem)
    prev_copy.start()

    barrier = pltpu.get_barrier_semaphore()

    def greet(k, carry):
        pl.semaphore_signal(
            barrier, inc=1, device_id={"gx": lax.rem(me + k, n)},
            device_id_type=pl.DeviceIdType.MESH,
        )
        return carry

    lax.fori_loop(1, n, greet, 0)

    zero_rows = jnp.zeros((2, width, PAD, nz), F32)
    for ref in (buf0, buf1, dz0, dz1):
        ref[:, :, pl.ds(0, PAD), :] = zero_rows
        ref[:, :, pl.ds(PAD + ny, PAD), :] = zero_rows
    zero_ends = jnp.zeros((2, 2, PAD, nz), F32)
    halo[:, :, pl.ds(0, PAD), :] = zero_ends
    halo[:, :, pl.ds(PAD + ny, PAD), :] = zero_ends
    for side, has in ((0, has_low), (1, has_high)):
        @pl.when(jnp.logical_not(has))
        def _(side=side):
            halo[side, :, rows, :] = jnp.zeros((2, ny, nz), F32)
            arrived[:, side] = jnp.zeros((STEPS - 1, 2, ny, nz), SEND)

    r = lax.broadcasted_iota(jnp.int32, (nz, 2 * nz), 0)
    c = lax.broadcasted_iota(jnp.int32, (nz, 2 * nz), 1)
    second = c < nz
    cz = jnp.where(second, c, c - nz)
    zmat[...] = jnp.where(
        r == cz + 1, 1.0,
        jnp.where(r == cz - 1, jnp.where(second, 1.0, -1.0),
                  jnp.where((r == cz) & second, -2.0, 0.0)),
    ).astype(jnp.bfloat16)

    def landing(step, side):
        return halo.at[side, :, rows, :] if step == 0 else arrived.at[step - 1, side]

    def halo_copy(step, side):
        if step == 0:
            src = now_hbm.at[:, 0 if side == 0 else width - 1]
        else:
            src = sendbuf.at[step - 1, side]
        return pltpu.make_async_remote_copy(
            src_ref=src,
            dst_ref=landing(step, 1 - side),
            send_sem=hs_sems.at[step, side],
            recv_sem=hr_sems.at[step, 1 - side],
            device_id={"gx": me - 1 if side == 0 else me + 1},
            device_id_type=pl.DeviceIdType.MESH,
        )

    def halo_arrived(step, side):
        return pltpu.make_async_remote_copy(
            src_ref=landing(step, side),
            dst_ref=landing(step, side),
            send_sem=hs_sems.at[step, side],
            recv_sem=hr_sems.at[step, side],
            device_id={"gx": me - 1 if side == 0 else me + 1},
            device_id_type=pl.DeviceIdType.MESH,
        )

    def send_halo(step):
        for side, has in ((0, has_low), (1, has_high)):
            @pl.when(has)
            def _(side=side):
                halo_copy(step, side).start()

    def z_terms(p):
        return jnp.dot(p.astype(jnp.bfloat16), zmat[...], preferred_element_type=F32)

    def prepare(x, carry):
        found = z_terms(buf0[:, x, rows, :].reshape(2 * ny, nz))
        theta_s, theta_c = sin_cos(tilt[x].astype(F32))
        alpha_s, alpha_c = sin_cos(azi[x].astype(F32))
        speed = cou[x].astype(F32)
        e2 = eps[x].astype(F32) * 2.0
        scaled = speed * e2
        base = speed + scaled
        nx = theta_s * alpha_c
        nyy = theta_s * alpha_s
        sx = scaled * nx
        sy = scaled * nyy
        scz = scaled * theta_c
        mxx = base - sx * nx
        myy = base - sy * nyy
        coef[0, x] = mxx
        coef[1, x] = myy
        coef[2, x] = base - scz * theta_c
        coef[3, x] = -0.5 * (sx * nyy)
        coef[4, x] = -0.5 * (scz * nx)
        coef[5, x] = -0.5 * (scz * nyy)
        coef[6, x] = 2.0 - 2.0 * (mxx + myy)
        sz0[:, x, rows, :] = found[:, :nz].reshape(2, ny, nz)
        dz0[:, x, rows, :] = found[:, nz:].reshape(2, ny, nz)
        return carry

    for g in range(GROUPS):
        for copy in group_copies(g):
            copy.wait()
        lax.fori_loop(g * group, (g + 1) * group, prepare, 0, unroll=4)
        if g == 0:
            pl.semaphore_wait(barrier, n - 1)
            send_halo(0)
    prev_copy.wait()

    def combine(cs, p, old, px, sy, sz, yx, dzx, dzy):
        acc = cs[6] * p - old
        acc += cs[0] * px + cs[1] * sy
        acc += cs[2] * sz + cs[3] * yx
        acc += cs[4] * dzx + cs[5] * dzy
        return acc

    def edges(step):
        now, prv = bufs[step % 2], bufs[(step + 1) % 2]
        sz, dz = szs[step % 2], dzs[step % 2]
        for side, has in ((0, has_low), (1, has_high)):
            @pl.when(has)
            def _(side=side):
                halo_arrived(step, side).wait_recv()
        if step == 0:
            both = halo[:, :, rows, :].reshape(4 * ny, nz).astype(jnp.bfloat16)
        else:
            both = arrived[step - 1].reshape(4 * ny, nz)
        outer = jnp.dot(both, zmat[:, nz:], preferred_element_type=F32)
        if step > 0:
            halo[:, :, rows, :] = arrived[step - 1].astype(F32)
        for side in range(2):
            x = 0 if side == 0 else width - 1
            inner = 1 if side == 0 else width - 2
            for y in range(0, ny, EDGE):
                mid, up, dn = [pl.ds(PAD + y + d, EDGE) for d in (0, 1, -1)]
                cs = [coef[k, x, pl.ds(y, EDGE), :] for k in range(7)]
                for f in range(2):
                    a = halo[side, f, mid, :]
                    ya = halo[side, f, up, :] - halo[side, f, dn, :]
                    first = (side * 2 + f) * ny + y
                    za = outer[first : first + EDGE]
                    b = now[f, inner, mid, :]
                    yb = now[f, inner, up, :] - now[f, inner, dn, :]
                    zb = dz[f, inner, mid, :]
                    acc = combine(
                        cs, now[f, x, mid, :], prv[f, x, mid, :], a + b,
                        now[f, x, up, :] + now[f, x, dn, :], sz[f, x, mid, :],
                        yb - ya if side == 0 else ya - yb,
                        zb - za if side == 0 else za - zb,
                        dz[f, x, up, :] - dz[f, x, dn, :],
                    )
                    prv[f, x, mid, :] = acc
                    if step < STEPS - 1:
                        sendbuf[step, side, f, pl.ds(y, EDGE), :] = acc.astype(SEND)
        if step < STEPS - 1:
            send_halo(step + 1)

    def inside(step, base, emit, tall):
        now, prv = bufs[step % 2], bufs[(step + 1) % 2]
        sz, dz = szs[step % 2], dzs[step % 2]
        mid, up, dn = [pl.ds(base + PAD + d, tall) for d in (0, 1, -1)]
        here = pl.ds(base, tall)
        p0, y0, d0, p1, y1, s1, d1 = [[None, None] for _ in range(7)]
        for f in range(2):
            p0[f] = now[f, 0, mid, :]
            y0[f] = now[f, 0, up, :] - now[f, 0, dn, :]
            d0[f] = dz[f, 0, mid, :]
            hi, lo = now[f, 1, up, :], now[f, 1, dn, :]
            p1[f], y1[f], s1[f], d1[f] = now[f, 1, mid, :], hi - lo, hi + lo, dz[f, 1, mid, :]
        for x in range(1, width - 1):
            cs = [coef[k, x, here, :] for k in range(7)]
            for f in range(2):
                hi, lo = now[f, x + 1, up, :], now[f, x + 1, dn, :]
                p2, y2, s2, d2 = now[f, x + 1, mid, :], hi - lo, hi + lo, dz[f, x + 1, mid, :]
                acc = combine(
                    cs, p1[f], prv[f, x, mid, :], p2 + p0[f], s1[f], sz[f, x, mid, :],
                    y2 - y0[f], d2 - d0[f], dz[f, x, up, :] - dz[f, x, dn, :],
                )
                emit(f, x, mid, acc)
                p0[f], y0[f], d0[f] = p1[f], y1[f], d1[f]
                p1[f], y1[f], s1[f], d1[f] = p2, y2, s2, d2

    def z_rows(step, base):
        prv, sz, dz = bufs[(step + 1) % 2], szs[(step + 1) % 2], dzs[(step + 1) % 2]
        at = pl.ds(base, TALL)
        found = z_terms(jnp.concatenate([prv[f, x, at, :] for x in range(width) for f in range(2)], axis=0))
        for x in range(width):
            for f in range(2):
                first = (x * 2 + f) * TALL
                sz[f, x, at, :] = found[first : first + TALL, :nz]
                dz[f, x, at, :] = found[first : first + TALL, nz:]

    for step in range(STEPS - 1):
        edges(step)

        def emit(f, x, mid, acc, prv=bufs[(step + 1) % 2]):
            prv[f, x, mid, :] = acc

        def advance(k, carry, step=step, emit=emit):
            base = pl.multiple_of(k * TALL, TALL)
            z_rows(step, base + PAD - TALL)
            inside(step, base, emit, TALL)
            return carry

        lax.fori_loop(0, ny // TALL, advance, 0)
        z_rows(step, PAD + ny - TALL)

    edges(STEPS - 1)
    final = bufs[STEPS % 2]
    span = jr * half
    each = n // chunks

    def piece(target, source):
        start = pl.multiple_of(((target * cols_per) // nz) * half, half)
        return pltpu.make_async_remote_copy(
            src_ref=snap_send.at[:, pl.ds(start, span), :],
            dst_ref=cols_ref.at[source],
            send_sem=as_sems.at[target],
            recv_sem=ar_sems.at[source],
            device_id={"gx": target},
            device_id_type=pl.DeviceIdType.MESH,
        )

    start = pl.multiple_of(((me * cols_per) // nz) * half, half)
    own = pltpu.make_async_copy(snap_send.at[:, pl.ds(start, span), :], cols_ref.at[me], own_sem)

    def last(k, carry):
        mine = me // each
        low = 2 * mine < chunks
        near = jnp.where(low, mine, chunks - 1 - mine)
        lead = chunks - 1 - 2 * near
        rest = jnp.maximum(k - lead, 0)
        pick = jnp.where(lax.rem(rest, 2) == 0, 2 * near - rest // 2, rest // 2)
        pick = jnp.where(k < lead, chunks - 1 - k, pick)
        block = jnp.where(low, pick, chunks - 1 - pick)
        base = pl.multiple_of(block * ROWS, ROWS)
        mid = pl.ds(base + PAD, ROWS)
        held = [final[f, 0, mid, :] for f in range(2)]

        def emit(f, x, mid, acc):
            if x % 2 == 0:
                held[f] = acc
            else:
                pair[f, pl.ds((x // 2) * ROWS, ROWS), :] = held[f] + acc

        inside(STEPS - 1, base, emit, ROWS)
        for f in range(2):
            pair[f, pl.ds((half - 1) * ROWS, ROWS), :] = held[f] + final[f, width - 1, mid, :]
        for f in range(2):
            for j in range(ROWS // 2):
                even = pair[f, pl.ds(2 * j, half, stride=ROWS), :]
                odd = pair[f, pl.ds(2 * j + 1, half, stride=ROWS), :]
                at = pl.multiple_of((block * (ROWS // 2) + j) * half, half)
                snap_send[f, pl.ds(at, half), :] = ((even + odd) * 0.25).astype(SEND)

        def send(u, carry):
            target = block * each + u

            @pl.when(target != me)
            def _():
                piece(target, me).start()

            return carry

        lax.fori_loop(0, each, send, 0)
        return carry

    lax.fori_loop(0, chunks, last, 0)
    own.start()

    for step in range(STEPS):
        for side, has in ((0, has_low), (1, has_high)):
            @pl.when(has)
            def _(step=step, side=side):
                halo_copy(step, side).wait_send()

    def wait_piece(k, carry):
        piece(lax.rem(me + k, n), me).wait_send()
        piece(lax.rem(me + k, n), lax.rem(me + k, n)).wait_recv()
        return carry

    lax.fori_loop(1, n, wait_piece, 0)
    own.wait()


def image_kernel(
    cols_per, jr, depth, offsets, tables_at, cols_ref, tab_ref, out_ref, lines, wide, keep, *prods
):
    n = cols_ref.shape[0]
    half = cols_ref.shape[2] // jr
    nz = cols_ref.shape[3]
    full = n * half
    step = pl.program_id(0)
    tables = tab_ref.shape[0]
    angles = tab_ref.shape[1]
    lags = tab_ref.shape[2]

    @pl.when(step == 0)
    def _():
        for f in range(2):
            for j in range(jr):
                for t in range(full // nz):
                    per = nz // half
                    block = cols_ref[pl.ds(t * per, per), f, pl.ds(j * half, half), :]
                    block = block.reshape(nz, nz).astype(F32)
                    lines[f, j, :, pl.ds(t * nz, nz)] = block.T.astype(SEND)
        lag = lax.broadcasted_iota(jnp.int32, (lags, lags * 8), 0)
        col = lax.broadcasted_iota(jnp.int32, (lags, lags * 8), 1)
        spread = jnp.where(col // 8 == lag, 1.0, 0.0).astype(jnp.bfloat16)
        flat = tab_ref[...].reshape(tables * angles, lags)
        wide[...] = jnp.dot(flat, spread, preferred_element_type=F32).astype(jnp.bfloat16)
        row_c = lax.rem(lax.broadcasted_iota(jnp.int32, (angles * 8, lags * 8), 0), 8)
        col_c = lax.rem(lax.broadcasted_iota(jnp.int32, (angles * 8, lags * 8), 1), 8)
        keep[...] = jnp.where(row_c == col_c, 1.0, 0.0).astype(jnp.bfloat16)

    me = lax.axis_index("gx")
    z0 = lax.rem(me * cols_per, nz)
    tiles = full // nz
    ta = tables * angles

    sub = lax.broadcasted_iota(jnp.int32, (8, ta), 0)
    lane_ta = lax.broadcasted_iota(jnp.int32, (angles, 8, ta), 2)
    row_a = lax.broadcasted_iota(jnp.int32, (angles, 8, ta), 0)
    weights = []
    for q in range(depth // 8):
        row0 = z0 + step * depth + q * 8
        chosen = jnp.zeros((8, ta), jnp.int32)
        for c in range(8):
            chosen = jnp.where(sub == c, tables_at[row0 + c], chosen)
        wanted = (chosen * angles)[None] + row_a
        pick = jnp.where(lane_ta == wanted, 1.0, 0.0).reshape(angles * 8, ta)
        dense = jnp.dot(pick.astype(jnp.bfloat16), wide[...], preferred_element_type=F32)
        weights.append(dense.astype(jnp.bfloat16) * keep[...])

    lane = lax.broadcasted_iota(jnp.int16, (depth, nz), 1)
    zero = jnp.zeros((depth, nz), SEND)

    def moved(parts, d):
        if d == 0:
            return parts
        turned = [pltpu.roll(part, d % nz, axis=1) for part in parts]
        if d > 0:
            return [
                jnp.where(lane >= d, turned[t], turned[t - 1] if t else zero)
                for t in range(tiles)
            ]
        return [
            jnp.where(lane < nz + d, turned[t], turned[t + 1] if t + 1 < tiles else zero)
            for t in range(tiles)
        ]

    row0 = pl.multiple_of(z0 + step * depth, depth)
    for j in range(jr):
        source = [lines[0, j, pl.ds(row0, depth), pl.ds(t * nz, nz)] for t in range(tiles)]
        receiver = [lines[1, j, pl.ds(row0, depth), pl.ds(t * nz, nz)] for t in range(tiles)]
        for d in range(-LAG_REACH, LAG_REACH):
            left, right = moved(source, d), moved(receiver, -d)
            for t in range(tiles):
                product = (left[t] * right[t]).astype(F32)
                for q in range(depth // 8):
                    prods[j * (depth // 8) + q][d + LAG_REACH, :, pl.ds(t * nz, nz)] = product[8 * q : 8 * q + 8]

        results = []
        for q in range(depth // 8):
            lagged = jnp.concatenate(
                [prods[j * (depth // 8) + q][offsets[h] + LAG_REACH] for h in range(lags)], axis=0
            ).astype(jnp.bfloat16)
            total = jnp.dot(weights[q], lagged, preferred_element_type=F32)
            results.append(total.reshape(angles, 8, full))
        out_ref[:, j] = jnp.concatenate(results, axis=1).astype(jnp.bfloat16)


def local(
    waves_now, waves_prev, epsilon, tilt, azimuth, courant, lag_offsets, table_index, lag_tables
):
    n = lax.axis_size("gx")
    width, ny, nz = epsilon.shape
    half = width // 2
    columns = (ny // 2) * nz
    cols_per = columns // n
    jr = max(1, cols_per // nz)
    full = n * half
    plane = (2, width, ny + 2 * PAD, nz)
    dma = pltpu.SemaphoreType.DMA
    cols = pl.pallas_call(
        functools.partial(wave_kernel, n, jr, cols_per),
        out_shape=jax.ShapeDtypeStruct((n, 2, jr * half, nz), SEND),
        in_specs=[pl.BlockSpec(memory_space=pltpu.HBM)] * 6,
        out_specs=pl.BlockSpec(memory_space=pl.ANY),
        scratch_shapes=[
            pltpu.VMEM(plane, F32),
            pltpu.VMEM(plane, F32),
            pltpu.VMEM(plane, F32),
            pltpu.VMEM(plane, F32),
            pltpu.VMEM(plane, F32),
            pltpu.VMEM(plane, F32),
            pltpu.VMEM((width, ny, nz), epsilon.dtype),
            pltpu.VMEM((width, ny, nz), tilt.dtype),
            pltpu.VMEM((width, ny, nz), azimuth.dtype),
            pltpu.VMEM((width, ny, nz), courant.dtype),
            pltpu.VMEM((7, width, ny, nz), F32),
            pltpu.VMEM((nz, 2 * nz), jnp.bfloat16),
            pltpu.VMEM((2, half * ROWS, nz), F32),
            pltpu.VMEM((2, (ny // 2) * half, nz), SEND),
            pltpu.VMEM((STEPS - 1, 2, 2, ny, nz), SEND),
            pltpu.VMEM((2, 2, ny + 2 * PAD, nz), F32),
            pltpu.VMEM((STEPS - 1, 2, 2, ny, nz), SEND),
            dma((GROUPS, 5)),
            dma,
            dma,
            dma((STEPS, 2)),
            dma((STEPS, 2)),
            dma((n,)),
            dma((n,)),
        ],
        compiler_params=pltpu.CompilerParams(
            collective_id=0, has_side_effects=True, vmem_limit_bytes=60 << 20
        ),
        name="waves",
    )(waves_now, waves_prev, epsilon, tilt, azimuth, courant)

    angles, lags = lag_tables.shape[1:]
    tables = lag_tables.shape[0]
    cz = min(cols_per, nz)
    depth = min(DEPTH, cz)
    image = pl.pallas_call(
        functools.partial(image_kernel, cols_per, jr, depth),
        grid=(cz // depth,),
        out_shape=jax.ShapeDtypeStruct((angles, jr, cz, full), jnp.bfloat16),
        in_specs=[
            pl.BlockSpec(memory_space=pltpu.SMEM),
            pl.BlockSpec(memory_space=pltpu.SMEM),
            pl.BlockSpec(memory_space=pltpu.VMEM),
            pl.BlockSpec(memory_space=pltpu.VMEM),
        ],
        out_specs=pl.BlockSpec((angles, jr, depth, full), lambda g: (0, 0, g, 0)),
        scratch_shapes=[
            pltpu.VMEM((2, jr, nz, full), SEND),
            pltpu.VMEM((tables * angles, lags * 8), jnp.bfloat16),
            pltpu.VMEM((angles * 8, lags * 8), jnp.bfloat16),
        ] + [pltpu.VMEM((2 * LAG_REACH, 8, full), F32)] * (jr * (depth // 8)),
        compiler_params=pltpu.CompilerParams(vmem_limit_bytes=60 << 20),
        name="image",
    )(lag_offsets, table_index, cols, lag_tables)
    return image.reshape(angles, cols_per, full)


def solution(mesh):
    wave = P(None, ("shot", "gx"), None, None)
    cell = P("gx", None, None)
    return jax.shard_map(
        local,
        mesh=mesh,
        in_specs=(wave, wave, cell, cell, cell, cell, P(), P(), P()),
        out_specs=P(None, ("shot", "gx"), None),
        check_vma=False,
    )
```
